256 devices in a mesh: seq: 64 (over x, z, core), tp: 4 (over y).
Axes of the slice: x: 4, y: 4, z: 8, core: 2. Of those that a mesh axis runs over, the one named last changes fastest.
Arguments:
- hidden_in: bfloat16 [16384, 1536], P('seq', 'tp'), may hold values from -6 to 6
- w_in_gate: float32 [1536, 3072], P('seq', 'tp'), may hold values from -0.15625 to 0.15625
- w_in_value: float32 [1536, 3072], P('seq', 'tp'), may hold values from -0.15625 to 0.15625
- w_in_shared: float32 [1536, 256], P('seq'), may hold values from -0.15625 to 0.15625
- w_in_step: float32 [1536, 48], P('seq', 'tp'), may hold values from -0.15625 to 0.15625
- conv_value: float32 [4, 3072], P(None, 'tp'), may hold values from -3 to 3
- conv_shared: float32 [4, 256], replicated, may hold values from -3 to 3
- dt_bias: float32 [48], P('tp'), may hold values from -4 to -2
- a_log: float32 [48], P('tp'), may hold values from -8 to 0
- skip_gain: float32 [48], P('tp'), may hold values from 0.6 to 4.8
- norm_gain: float32 [3072], P('tp'), may hold values from 0.1 to 1.9
- w_out: float32 [3072, 1536], P('tp', 'seq'), may hold values from -0.109375 to 0.109375
- prompt_lengths: int32 [8], replicated, may hold values from 1 to 8192, 16384 in all
- row_blocks: int32 [64], replicated, may hold values from 0 to 63, each once
Outputs:
- mixed_out: bfloat16 [16384, 1536], P('seq', 'tp')
The draws below stay inside these ranges and needn't reach their ends.
Inputs may be any that keep to these rules, and one draw needn't show every extreme that they name: `prompt_lengths`: 8 lengths that sum to 16384, the longest exactly 8192. `row_blocks`: a permutation of the row blocks.
All inputs are finite; a program needn't handle non-finite values.
Results may differ from the reference program's by a relative error of at most 0.02.
Values may be sent and summed in bfloat16 or wider, within the bound.
No kernel may reach another device: no remote copies, remote signals or barrier semaphores. Data moves between devices by JAX's collectives and lax.ppermute only.
A program may use at most 128 MiB of HBM per device.

```python
import math
import jax
import jax.numpy as jnp
import numpy as np
from jax import lax

D = 1536
HEADS = 48
HEADDIM = 64
STATE = 128
KCONV = 4
SPAN = 256
PROMPTS = 8
INNER = 3072
TOKENS = 16384
MOST = 8192
ROW_BLOCKS = 64


def draw_a_log(key, part):
    first_key, second_key, third_key = jax.random.split(key, 3)
    quick_heads = jax.random.uniform(first_key, (HEADS,)) < 0.5
    quick_rate = jnp.log(jax.random.uniform(second_key, (HEADS,), minval=0.3, maxval=0.8))
    slow_rate = jnp.log(jax.random.uniform(third_key, (HEADS,), minval=12.0, maxval=40.0) / MOST)
    return jnp.where(quick_heads, quick_rate, slow_rate).astype(jnp.float32)


def draw_skip_gain(key, part):
    rising = 1.0 + 2.0 * jnp.arange(HEADS, dtype=jnp.float32) / (HEADS - 1)
    spread = jax.random.uniform(key, (HEADS,), minval=0.8, maxval=1.25)
    return (rising * spread).astype(jnp.float32)


def block_scale(stream_key, extent, cuts, low, high):
    factor_of = 1.0
    for axis_at, parts in cuts:
        steps = jax.random.uniform(jax.random.fold_in(jax.random.fold_in(stream_key, 6), axis_at), (parts,), jnp.float32, low / len(cuts), high / len(cuts))
        factor_of = factor_of * jnp.repeat(jnp.exp(steps), extent[axis_at] // parts).reshape((-1,) + (1,) * (len(extent) - 1 - axis_at))
    return factor_of


def length_profile(amount, total, limit, slope):
    loads = [(1 << 20) // math.isqrt(grade ** slope) + 1 for grade in range(2, amount + 1)]
    surplus, holding = total - limit - (amount - 1), [1] * (amount - 1)
    while surplus > 0:
        candidates = [i for i in range(amount - 1) if holding[i] < limit]
        mass, left = sum([loads[i] for i in candidates]), surplus
        for i in candidates:
            extra = min(limit - holding[i], max(1, left * loads[i] // mass), surplus)
            holding[i] = holding[i] + extra
            surplus = surplus - extra
    return np.array([limit] + holding)


def ragged(key, count, total, most, slope):
    if count == 2:
        one = jax.random.randint(key, (), max(1, total - most), min(most, total - 1) + 1)
        return jnp.stack([one, total - one])
    lengths = jnp.asarray(length_profile(count, total, most, slope), jnp.int32)
    twos = (count - 1) // 2
    donor, taker = lengths[1:1 + 2 * twos:2], lengths[2:2 + 2 * twos:2]
    margin = jnp.minimum(donor - 1, most - taker)
    passed = jax.random.randint(jax.random.fold_in(key, 1), (twos,), 0, 1 << 20) % (margin + 1)
    lengths = lengths.at[1:1 + 2 * twos:2].set(donor - passed).at[2:2 + 2 * twos:2].set(taker + passed)
    return lengths[jax.random.permutation(jax.random.fold_in(key, 2), count)]


def normal_values(stream_key, shape, scale, reach, cuts=(), kind=jnp.bfloat16):
    loudness = block_scale(stream_key, shape, cuts, -0.22, 0.18) if cuts else 1.0
    drawn = jax.random.normal(stream_key, shape, jnp.float32) * scale * loudness
    return jnp.minimum(jnp.maximum(drawn, -reach), reach).astype(kind)


def setup_inputs(seed: int = 0) -> dict:
    splits = jax.random.split(jax.random.key(seed), 15)
    return {
        "hidden_in": normal_values(splits[0], (TOKENS, D), 1.0, 6.0, ((0, 64), (1, 4))),
        "w_in_gate": normal_values(splits[1], (D, INNER), D ** -0.5, 0.15625, ((0, 64), (1, 4)), jnp.float32),
        "w_in_value": normal_values(splits[2], (D, INNER), D ** -0.5, 0.15625, ((0, 64), (1, 4)), jnp.float32),
        "w_in_shared": normal_values(splits[3], (D, 2 * STATE), D ** -0.5, 0.15625, ((0, 64),), jnp.float32),
        "w_in_step": normal_values(splits[4], (D, HEADS), D ** -0.5, 0.15625, ((0, 64), (1, 4)), jnp.float32),
        "conv_value": normal_values(splits[5], (KCONV, INNER), 0.5, 3.0, ((1, 4),), jnp.float32),
        "conv_shared": normal_values(splits[6], (KCONV, 2 * STATE), 0.5, 3.0, (), jnp.float32),
        "dt_bias": jnp.clip(-4.0 + 2.0 * jax.random.uniform(splits[7], (HEADS,), jnp.float32) ** block_scale(splits[7], (HEADS,), ((0, 4),), -0.2, 0.2), -4.0, -2.0),
        "a_log": draw_a_log(jax.random.fold_in(splits[14], 71), 0),
        "skip_gain": draw_skip_gain(jax.random.fold_in(splits[14], 71), 0),
        "norm_gain": jnp.clip(1.0 + 0.18 * jax.random.normal(splits[10], (INNER,), jnp.float32), 0.1, 1.9),
        "w_out": normal_values(splits[11], (INNER, D), INNER ** -0.5, 0.109375, ((0, 4), (1, 64)), jnp.float32),
        "prompt_lengths": ragged(splits[12], PROMPTS, TOKENS, MOST, 2).astype(jnp.int32),
        "row_blocks": jax.random.permutation(splits[13], ROW_BLOCKS).astype(jnp.int32),
    }


EPSILON = 1e-05
HIGHEST_PREC = lax.Precision.HIGHEST

def segment_of(positions, doc_ends):
    return lax.optimization_barrier(jnp.sum((positions[:, None] >= doc_ends[None, :]).astype(jnp.int32), axis=1))

def span_parts(values, b_half, c_half, steps_dt, decay_rates, segments, prev_seg):
    length = values.shape[0]
    b_rows = b_half.astype(jnp.float32)
    cumulative = jnp.cumsum(-steps_dt * decay_rates[None, :], axis=0)
    places = jnp.arange(length)
    causal = (places[:, None] >= places[None, :]) & (segments[:, None] == segments[None, :])
    gaps_log = jnp.where(causal[:, :, None], cumulative[:, None, :] - cumulative[None, :, :], 0.0)
    decays_in = jnp.where(causal[:, :, None], jnp.exp(gaps_log), 0.0)
    scores = jnp.dot(c_half, b_half.T, preferred_element_type=jnp.float32)
    weights = scores[:, :, None] * decays_in * steps_dt[None, :, :]
    intra_part = jnp.einsum('ijh,jhp->ihp', weights, values, precision=HIGHEST_PREC)
    carry_in = jnp.where((segments == prev_seg)[:, None], jnp.exp(cumulative), 0.0)
    tail_weight = jnp.where((segments == segments[-1])[:, None], jnp.exp(cumulative[-1][None, :] - cumulative), 0.0) * steps_dt
    fresh_state = jnp.einsum('jh,jhp,jn->hpn', tail_weight, values, b_rows, precision=HIGHEST_PREC)
    keep_factor = jnp.where(segments[-1] == prev_seg, jnp.exp(cumulative[-1]), 0.0)
    return (intra_part, carry_in, fresh_state, keep_factor)

def reference(hidden_in, w_in_gate, w_in_value, w_in_shared, w_in_step, conv_value, conv_shared, dt_bias, a_log, skip_gain, norm_gain, w_out, prompt_lengths, row_blocks):
    inverse_order = jnp.argsort(row_blocks).astype(jnp.int32)

    def model_rows(stored):
        blocks = stored.reshape(ROW_BLOCKS, D // ROW_BLOCKS, stored.shape[1])
        return jnp.take(blocks, inverse_order, axis=0).reshape(D, stored.shape[1]).astype(jnp.bfloat16)
    w_all = jnp.concatenate([model_rows(matrix) for matrix in (w_in_gate, w_in_value, w_in_shared, w_in_step)], axis=1)
    kernel = jnp.concatenate([conv_value, conv_shared], axis=1)
    doc_ends = jnp.cumsum(prompt_lengths).astype(jnp.int32)
    decay_rates = jnp.exp(a_log)
    out_weight = w_out.astype(jnp.bfloat16)
    span_count = TOKENS // SPAN
    edge_count = KCONV - 1
    mix_width = INNER + 2 * STATE

    def one_block(carried, inputs):
        state_in, edge_rows = carried
        block_index, block_rows = inputs
        first_pos = block_index * SPAN
        positions = first_pos + jnp.arange(SPAN, dtype=jnp.int32)
        projected = jnp.dot(block_rows, w_all, preferred_element_type=jnp.float32).astype(jnp.bfloat16)
        gate_rows = projected[:, :INNER]
        mixed_in = projected[:, INNER:INNER + mix_width]
        raw_step = projected[:, INNER + mix_width:]
        segments = segment_of(positions, doc_ends)
        edge_positions = first_pos - edge_count + jnp.arange(edge_count, dtype=jnp.int32)
        ext_segments = jnp.concatenate([segment_of(edge_positions, doc_ends), segments])
        ext_rows = jnp.concatenate([edge_rows, mixed_in], axis=0)
        conv_sum = jnp.zeros((SPAN, mix_width), jnp.float32)
        for tap_index in range(KCONV):
            same_doc = (ext_segments[tap_index:tap_index + SPAN] == segments)[:, None]
            conv_sum = conv_sum + jnp.where(same_doc, kernel[tap_index][None, :] * ext_rows[tap_index:tap_index + SPAN].astype(jnp.float32), 0.0)
        convolved = jax.nn.silu(conv_sum).astype(jnp.bfloat16)
        values = convolved[:, :INNER].astype(jnp.float32).reshape(SPAN, HEADS, HEADDIM)
        b_half = convolved[:, INNER:INNER + STATE]
        c_half = convolved[:, INNER + STATE:]
        c_rows = c_half.astype(jnp.float32)
        steps_dt = jax.nn.softplus(raw_step.astype(jnp.float32) + dt_bias[None, :])
        prev_seg = segment_of(positions[:1] - 1, doc_ends)[0]
        intra_part, carry_in, fresh_state, keep_factor = span_parts(values, b_half, c_half, steps_dt, decay_rates, segments, prev_seg)
        inter_part = jnp.einsum('in,hpn->ihp', c_rows, state_in, precision=HIGHEST_PREC) * carry_in[:, :, None]
        outputs = intra_part + inter_part + skip_gain[None, :, None] * values
        gated = outputs.reshape(SPAN, INNER) * jax.nn.silu(gate_rows.astype(jnp.float32))
        mean_square = lax.optimization_barrier(jnp.sum(gated * gated, axis=1)) / INNER
        normed = (gated * lax.rsqrt(mean_square + EPSILON)[:, None] * norm_gain[None, :]).astype(jnp.bfloat16)
        out_rows = jnp.dot(normed, out_weight, preferred_element_type=jnp.float32).astype(jnp.bfloat16)
        state_out = keep_factor[:, None, None] * state_in + fresh_state
        return ((state_out, mixed_in[SPAN - edge_count:]), out_rows)
    initial = (jnp.zeros((HEADS, HEADDIM, STATE), jnp.float32), jnp.zeros((edge_count, mix_width), jnp.bfloat16))
    blocks_in = (jnp.arange(span_count, dtype=jnp.int32), hidden_in.reshape(span_count, SPAN, D))
    last_carry, outputs = lax.scan(one_block, initial, blocks_in)
    return outputs.reshape(TOKENS, D)
```

```python
import jax
import jax.numpy as jnp
from jax import lax
from jax.experimental import pallas as pl
from jax.experimental.pallas import tpu as pltpu
from jax.sharding import Mesh, PartitionSpec as P

EPSILON = 1e-05
EDGE = 8
SEQ = ("x", "z", "core")
SIZES = (4, 8, 2)
BF16 = jnp.bfloat16
F32 = jnp.float32


def ahead(block, axis, distance):
    count = lax.axis_size(axis)
    return lax.ppermute(block, axis, [(i, (i + distance) % count) for i in range(count)])


def segment_of(positions, doc_ends):
    return jnp.sum((positions[:, None] >= doc_ends[None, :]).astype(jnp.int32), axis=1)


def scan_body(count, heads, sent_ref, out_ref):
    keeps = sent_ref[:, heads, :].astype(F32) + sent_ref[:, heads + 1, :].astype(F32)
    keeps = keeps.T
    rows = sent_ref.shape[1]
    carried = jnp.zeros((rows, keeps.shape[0]), F32)
    for k in range(count):
        out_ref[k] = carried.astype(BF16)
        keep = keeps[:rows, k : k + 1]
        carried = keep * carried + sent_ref[k].astype(F32)


def scan_states(sent, heads):
    count = sent.shape[0]
    return pl.pallas_call(
        lambda sent_ref, out_ref: scan_body(count, heads, sent_ref, out_ref),
        out_shape=jax.ShapeDtypeStruct(sent.shape, BF16),
        in_specs=[pl.BlockSpec(memory_space=pltpu.VMEM)],
        out_specs=pl.BlockSpec(memory_space=pltpu.VMEM),
        cost_estimate=pl.CostEstimate(
            flops=2 * sent.size, bytes_accessed=4 * sent.size, transcendentals=0
        ),
    )(sent)


def on_device(
    hidden_in,
    w_in_gate,
    w_in_value,
    w_in_shared,
    w_in_step,
    conv_value,
    conv_shared,
    dt_bias,
    a_log,
    skip_gain,
    norm_gain,
    w_out,
    prompt_lengths,
    row_blocks,
):
    x_size, z_size, core_size = SIZES
    seq_count = x_size * z_size * core_size
    tp_count = lax.axis_size("tp")
    tokens, features = hidden_in.shape
    rows_here, inner = w_in_value.shape
    shared = w_in_shared.shape[1]
    heads = dt_bias.shape[0]
    head_dim = inner // heads
    state = shared // 2
    x_at, z_at, core_at = (lax.axis_index(name) for name in SEQ)
    tp_at = lax.axis_index("tp")
    seq_at = (x_at * z_size + z_at) * core_size + core_at

    late = jnp.concatenate([w_in_gate.astype(BF16), w_out.T.astype(BF16)], axis=1)
    late = lax.all_gather(late, SEQ, axis=0, tiled=True)

    before = lax.ppermute(
        hidden_in[tokens - EDGE :], SEQ, [(i, i + 1) for i in range(seq_count - 1)]
    )
    mine = jnp.concatenate([before, hidden_in], axis=0)
    hidden = jnp.concatenate([mine] + [ahead(mine, "tp", d) for d in range(1, tp_count)], axis=1)

    spare = -(inner + shared + heads) % 128
    early = jnp.concatenate(
        [w_in_value, w_in_shared, w_in_step, jnp.zeros((rows_here, spare), F32)], axis=1
    ).astype(BF16)
    along_z = lax.all_gather(early, "z", axis=0, tiled=True)
    own = jnp.concatenate(
        [along_z] + [ahead(along_z, "x", d) for d in range(1, x_size)], axis=0
    )
    other = ahead(own, "core", 1)

    dx = jnp.arange(x_size, dtype=jnp.int32)[:, None]
    dz = jnp.arange(z_size, dtype=jnp.int32)[None, :]
    chips = (((x_at - dx) % x_size) * z_size + dz).reshape(-1) * core_size
    blocks_each = seq_count // tp_count

    def columns_for(stored):
        model = jnp.take(row_blocks, stored)
        piece = (tp_at - model // blocks_each) % tp_count
        place = piece * blocks_each + model % blocks_each
        cut = hidden.reshape(hidden.shape[0], seq_count, rows_here)
        return jnp.take(cut, place, axis=1).reshape(hidden.shape[0], -1)

    h_own = columns_for(chips + core_at)
    h_other = columns_for(chips + (1 - core_at))
    h_all = columns_for(jnp.arange(seq_count, dtype=jnp.int32))

    projected = (
        jnp.dot(h_own, own, preferred_element_type=F32)
        + jnp.dot(h_other, other, preferred_element_type=F32)
    ).astype(BF16)
    mixed = projected[:, : inner + shared]
    raw = projected[EDGE:, inner + shared : inner + shared + heads]

    doc_ends = jnp.cumsum(prompt_lengths)
    first = seq_at * tokens
    ext_segments = segment_of(first - EDGE + jnp.arange(EDGE + tokens, dtype=jnp.int32), doc_ends)
    segments = ext_segments[EDGE:]
    prev_seg = ext_segments[EDGE - 1]
    taps = jnp.concatenate([conv_value, conv_shared], axis=1)
    conv_sum = jnp.zeros((tokens, inner + shared), F32)
    width = taps.shape[0]
    for k in range(width):
        at = EDGE - width + 1 + k
        same = (ext_segments[at : at + tokens] == segments)[:, None]
        conv_sum = conv_sum + jnp.where(
            same, taps[k][None, :] * mixed[at : at + tokens].astype(F32), 0.0
        )
    convolved = jax.nn.silu(conv_sum).astype(BF16)
    values = convolved[:, :inner].reshape(tokens, heads, head_dim)
    b_half = convolved[:, inner : inner + state]
    c_half = convolved[:, inner + state :]
    steps = jax.nn.softplus(raw.astype(F32) + dt_bias[None, :])
    cumulative = jnp.cumsum(-steps * jnp.exp(a_log)[None, :], axis=0)

    tail = (
        jnp.where(
            (segments == segments[-1])[:, None], jnp.exp(cumulative[-1][None, :] - cumulative), 0.0
        )
        * steps
    )
    weighted = (tail[:, :, None] * values.astype(F32)).astype(BF16)
    fresh = lax.dot_general(
        weighted.reshape(tokens, inner), b_half, (((0,), (0,)), ((), ())), preferred_element_type=F32
    )
    keep = jnp.where(segments[-1] == prev_seg, jnp.exp(cumulative[-1]), 0.0)
    keep_hi = keep.astype(BF16)
    keep_lo = (keep - keep_hi.astype(F32)).astype(BF16)
    keep_rows = jnp.pad(jnp.stack([keep_hi, keep_lo]), ((0, 2), (0, state - heads)))
    sent = jnp.concatenate(
        [
            fresh.astype(BF16).reshape(heads, head_dim, state).transpose(1, 0, 2),
            jnp.broadcast_to(keep_rows[None], (head_dim,) + keep_rows.shape),
        ],
        axis=1,
    )
    received = lax.all_to_all(sent, SEQ, 0, 0, tiled=True)
    carried = lax.all_to_all(scan_states(received, heads), SEQ, 0, 0, tiled=True)
    carried = carried[:, :heads].transpose(1, 0, 2).reshape(inner, state)

    places = jnp.arange(tokens)
    causal = (places[:, None] >= places[None, :]) & (segments[:, None] == segments[None, :])
    scores = jnp.dot(c_half, b_half.T, preferred_element_type=F32)
    cum_t = cumulative.T
    gaps = jnp.where(causal[None], cum_t[:, :, None] - cum_t[:, None, :], -jnp.inf)
    weights = (scores[None] * jnp.exp(gaps) * steps.T[:, None, :]).astype(BF16)
    intra = jnp.einsum("hij,jhp->ihp", weights, values, preferred_element_type=F32)
    direct = intra + skip_gain[None, :, None] * values.astype(F32)
    carry_in = jnp.where((segments == prev_seg)[:, None], jnp.exp(cumulative), 0.0)

    gate = jnp.dot(h_all[EDGE:], late[:, :inner], preferred_element_type=F32).astype(BF16)
    inter = lax.dot_general(
        c_half, carried, (((1,), (1,)), ((), ())), preferred_element_type=F32
    ).reshape(tokens, heads, head_dim)
    mixed_heads = (direct + inter * carry_in[:, :, None]).reshape(tokens, inner)
    gated = mixed_heads * jax.nn.silu(gate.astype(F32))

    squares = jnp.sum(gated * gated, axis=1, keepdims=True)
    total = squares + sum(ahead(squares, "tp", d) for d in range(1, tp_count))
    scale = lax.rsqrt(total / (inner * tp_count) + EPSILON)
    terms = lax.dot_general(
        (gated * norm_gain[None, :]).astype(BF16),
        late[:, inner:],
        (((1,), (1,)), ((), ())),
        preferred_element_type=F32,
    ).astype(BF16)

    def share(d):
        return lax.dynamic_slice_in_dim(terms, ((tp_at + d) % tp_count) * features, features, 1)

    summed = share(0).astype(F32)
    for d in range(1, tp_count):
        summed = summed + ahead(share(d), "tp", d).astype(F32)
    return (summed * scale).astype(BF16)


def solution(mesh):
    fine = Mesh(mesh.devices.reshape(SIZES + (-1,)), SEQ + ("tp",))
    return jax.shard_map(
        on_device,
        mesh=fine,
        in_specs=(
            P(SEQ, "tp"),
            P(SEQ, "tp"),
            P(SEQ, "tp"),
            P(SEQ, None),
            P(SEQ, "tp"),
            P(None, "tp"),
            P(),
            P("tp"),
            P("tp"),
            P("tp"),
            P("tp"),
            P("tp", SEQ),
            P(),
            P(),
        ),
        out_specs=P(SEQ, "tp"),
        check_vma=False,
    )
```

```python
import jax
import jax.numpy as jnp
from jax import lax
from jax.experimental import pallas as pl
from jax.experimental.pallas import tpu as pltpu
from jax.sharding import Mesh, PartitionSpec as P

EPSILON = 1e-05
EDGE = 8
SEQ = ("x", "z", "core")
SIZES = (4, 8, 2)
BF16 = jnp.bfloat16
F32 = jnp.float32


def ahead(block, axis, distance):
    count = lax.axis_size(axis)
    return lax.ppermute(block, axis, [(i, (i + distance) % count) for i in range(count)])


def segment_of(positions, doc_ends):
    return jnp.sum((positions[:, None] >= doc_ends[None, :]).astype(jnp.int32), axis=1)


def scan_body(count, heads, sent_ref, out_ref):
    keeps = sent_ref[:, heads, :].astype(F32) + sent_ref[:, heads + 1, :].astype(F32)
    keeps = keeps.T
    rows = sent_ref.shape[1]
    carried = jnp.zeros((rows, keeps.shape[0]), F32)
    for k in range(count):
        out_ref[k] = carried.astype(BF16)
        keep = keeps[:rows, k : k + 1]
        carried = keep * carried + sent_ref[k].astype(F32)


def scan_states(sent, heads):
    count = sent.shape[0]
    return pl.pallas_call(
        lambda sent_ref, out_ref: scan_body(count, heads, sent_ref, out_ref),
        out_shape=jax.ShapeDtypeStruct(sent.shape, BF16),
        in_specs=[pl.BlockSpec(memory_space=pltpu.VMEM)],
        out_specs=pl.BlockSpec(memory_space=pltpu.VMEM),
        cost_estimate=pl.CostEstimate(
            flops=2 * sent.size, bytes_accessed=4 * sent.size, transcendentals=0
        ),
    )(sent)


def pack_body(value_ref, shared_ref, step_ref, out_ref):
    inner, shared, heads = value_ref.shape[1], shared_ref.shape[1], step_ref.shape[1]
    out_ref[:, :inner] = value_ref[...].astype(BF16)
    out_ref[:, inner : inner + shared] = shared_ref[...].astype(BF16)
    rest = out_ref.shape[1] - inner - shared
    step = jnp.pad(step_ref[...], ((0, 0), (0, rest - heads)))
    out_ref[:, inner + shared :] = step.astype(BF16)


def pack_early(value, shared, step):
    width = value.shape[1] + shared.shape[1] + step.shape[1]
    width += -width % 128
    return pl.pallas_call(
        pack_body,
        out_shape=jax.ShapeDtypeStruct((value.shape[0], width), BF16),
        in_specs=[pl.BlockSpec(memory_space=pltpu.VMEM)] * 3,
        out_specs=pl.BlockSpec(memory_space=pltpu.VMEM),
    )(value, shared, step)


def on_device(
    hidden_in,
    w_in_gate,
    w_in_value,
    w_in_shared,
    w_in_step,
    conv_value,
    conv_shared,
    dt_bias,
    a_log,
    skip_gain,
    norm_gain,
    w_out,
    prompt_lengths,
    row_blocks,
):
    x_size, z_size, core_size = SIZES
    seq_count = x_size * z_size * core_size
    tp_count = lax.axis_size("tp")
    tokens, features = hidden_in.shape
    rows_here, inner = w_in_value.shape
    shared = w_in_shared.shape[1]
    heads = dt_bias.shape[0]
    head_dim = inner // heads
    state = shared // 2
    x_at, z_at, core_at = (lax.axis_index(name) for name in SEQ)
    tp_at = lax.axis_index("tp")
    seq_at = (x_at * z_size + z_at) * core_size + core_at

    before = lax.ppermute(
        hidden_in[tokens - EDGE :], SEQ, [(i, i + 1) for i in range(seq_count - 1)]
    )
    early = pack_early(w_in_value, w_in_shared, w_in_step)

    late = jnp.concatenate([w_in_gate.astype(BF16), w_out.T.astype(BF16)], axis=1)
    late = lax.all_gather(late, SEQ, axis=0, tiled=True)

    half = z_size // 2
    pair = jnp.concatenate([early, ahead(early, "z", half)], axis=0)
    before, pair = lax.optimization_barrier((before, pair))
    mine = jnp.concatenate([before, hidden_in], axis=0)
    hidden = jnp.concatenate([mine] + [ahead(mine, "tp", d) for d in range(1, tp_count)], axis=1)
    z_shifts = [0, 1, 2, z_size - 1]
    along_z = jnp.concatenate([pair] + [ahead(pair, "z", d) for d in z_shifts[1:]], axis=0)
    z_offsets = [(d + o) % z_size for d in z_shifts for o in (0, half)]
    own = [along_z] + [ahead(along_z, "x", d) for d in range(1, x_size)]
    other = [ahead(block, "core", 1) for block in own]

    chips = [
        jnp.stack([((x_at - d) % x_size * z_size + (z_at - o) % z_size) for o in z_offsets])
        * core_size
        for d in range(x_size)
    ]
    blocks_each = seq_count // tp_count

    def columns_for(stored):
        model = jnp.take(row_blocks, stored)
        piece = (tp_at - model // blocks_each) % tp_count
        place = piece * blocks_each + model % blocks_each
        cut = hidden.reshape(hidden.shape[0], seq_count, rows_here)
        return jnp.take(cut, place, axis=1).reshape(hidden.shape[0], -1)

    h_all = columns_for(jnp.arange(seq_count, dtype=jnp.int32))
    order = [stored + core_at for stored in chips] + [stored + (1 - core_at) for stored in chips]
    h_early = columns_for(jnp.concatenate(order))
    depth = early.shape[0] * z_size
    projected = sum(
        jnp.dot(h_early[:, i * depth : (i + 1) * depth], block, preferred_element_type=F32)
        for i, block in enumerate(own + other)
    ).astype(BF16)
    mixed = projected[:, : inner + shared]
    raw = projected[EDGE:, inner + shared : inner + shared + heads]

    doc_ends = jnp.cumsum(prompt_lengths)
    first = seq_at * tokens
    ext_segments = segment_of(first - EDGE + jnp.arange(EDGE + tokens, dtype=jnp.int32), doc_ends)
    segments = ext_segments[EDGE:]
    prev_seg = ext_segments[EDGE - 1]
    taps = jnp.concatenate([conv_value, conv_shared], axis=1)
    conv_sum = jnp.zeros((tokens, inner + shared), F32)
    width = taps.shape[0]
    for k in range(width):
        at = EDGE - width + 1 + k
        same = (ext_segments[at : at + tokens] == segments)[:, None]
        conv_sum = conv_sum + jnp.where(
            same, taps[k][None, :] * mixed[at : at + tokens].astype(F32), 0.0
        )
    convolved = jax.nn.silu(conv_sum).astype(BF16)
    values = convolved[:, :inner].reshape(tokens, heads, head_dim)
    b_half = convolved[:, inner : inner + state]
    c_half = convolved[:, inner + state :]
    steps = jax.nn.softplus(raw.astype(F32) + dt_bias[None, :])
    cumulative = jnp.cumsum(-steps * jnp.exp(a_log)[None, :], axis=0)

    tail = (
        jnp.where(
            (segments == segments[-1])[:, None], jnp.exp(cumulative[-1][None, :] - cumulative), 0.0
        )
        * steps
    )
    weighted = (tail[:, :, None] * values.astype(F32)).astype(BF16)
    fresh = lax.dot_general(
        weighted.reshape(tokens, inner), b_half, (((0,), (0,)), ((), ())), preferred_element_type=F32
    )
    keep = jnp.where(segments[-1] == prev_seg, jnp.exp(cumulative[-1]), 0.0)
    keep_hi = keep.astype(BF16)
    keep_lo = (keep - keep_hi.astype(F32)).astype(BF16)
    keep_rows = jnp.pad(jnp.stack([keep_hi, keep_lo]), ((0, 2), (0, state - heads)))
    sent = jnp.concatenate(
        [
            fresh.astype(BF16).reshape(heads, head_dim, state).transpose(1, 0, 2),
            jnp.broadcast_to(keep_rows[None], (head_dim,) + keep_rows.shape),
        ],
        axis=1,
    )
    received = lax.all_to_all(sent, SEQ, 0, 0, tiled=True)
    carried = lax.all_to_all(scan_states(received, heads), SEQ, 0, 0, tiled=True)
    carried = carried[:, :heads].transpose(1, 0, 2).reshape(inner, state)

    places = jnp.arange(tokens)
    causal = (places[:, None] >= places[None, :]) & (segments[:, None] == segments[None, :])
    scores = jnp.dot(c_half, b_half.T, preferred_element_type=F32)
    cum_t = cumulative.T
    gaps = jnp.where(causal[None], cum_t[:, :, None] - cum_t[:, None, :], -jnp.inf)
    weights = (scores[None] * jnp.exp(gaps) * steps.T[:, None, :]).astype(BF16)
    intra = jnp.einsum("hij,jhp->ihp", weights, values, preferred_element_type=F32)
    direct = intra + skip_gain[None, :, None] * values.astype(F32)
    carry_in = jnp.where((segments == prev_seg)[:, None], jnp.exp(cumulative), 0.0)

    gate = jnp.dot(h_all[EDGE:], late[:, :inner], preferred_element_type=F32).astype(BF16)
    inter = lax.dot_general(
        c_half, carried, (((1,), (1,)), ((), ())), preferred_element_type=F32
    ).reshape(tokens, heads, head_dim)
    mixed_heads = (direct + inter * carry_in[:, :, None]).reshape(tokens, inner)
    gated = mixed_heads * jax.nn.silu(gate.astype(F32))

    squares = lax.dot_general(
        jnp.ones((1, inner), F32),
        gated * gated,
        (((1,), (1,)), ((), ())),
        precision=lax.Precision.HIGHEST,
        preferred_element_type=F32,
    )
    squares_hi = squares.astype(BF16)
    squares_lo = (squares - squares_hi.astype(F32)).astype(BF16)
    riding = jnp.concatenate([squares_hi, squares_lo], axis=0)
    riding = jnp.pad(riding, ((0, 6), (0, features - tokens)))
    terms = lax.dot_general(
        (gated * norm_gain[None, :]).astype(BF16),
        late[:, inner:],
        (((1,), (1,)), ((), ())),
        preferred_element_type=F32,
    ).astype(BF16)

    def share(d):
        cut = lax.dynamic_slice_in_dim(terms, ((tp_at + d) % tp_count) * features, features, 1)
        return jnp.concatenate([cut, riding], axis=0)

    parts = [share(0)] + [ahead(share(d), "tp", d) for d in range(1, tp_count)]
    summed = sum(part.astype(F32) for part in parts)
    total = summed[tokens, :tokens] + summed[tokens + 1, :tokens]
    scale = lax.rsqrt(total / (inner * tp_count) + EPSILON)
    return (summed[:tokens] * scale[:, None]).astype(BF16)


def solution(mesh):
    fine = Mesh(mesh.devices.reshape(SIZES + (-1,)), SEQ + ("tp",))
    return jax.shard_map(
        on_device,
        mesh=fine,
        in_specs=(
            P(SEQ, "tp"),
            P(SEQ, "tp"),
            P(SEQ, "tp"),
            P(SEQ, None),
            P(SEQ, "tp"),
            P(None, "tp"),
            P(),
            P("tp"),
            P("tp"),
            P("tp"),
            P("tp"),
            P("tp", SEQ),
            P(),
            P(),
        ),
        out_specs=P(SEQ, "tp"),
        check_vma=False,
    )
```

```python
import jax
import jax.numpy as jnp
from jax import lax
from jax.experimental import pallas as pl
from jax.experimental.pallas import tpu as pltpu
from jax.sharding import Mesh, PartitionSpec as P

EPSILON = 1e-05
EDGE = 8
SEQ = ("x", "z", "core")
SIZES = (4, 8, 2)
BF16 = jnp.bfloat16
F32 = jnp.float32


def ahead(block, axis, distance):
    count = lax.axis_size(axis)
    return lax.ppermute(block, axis, [(i, (i + distance) % count) for i in range(count)])


def segment_of(positions, doc_ends):
    return jnp.sum((positions[:, None] >= doc_ends[None, :]).astype(jnp.int32), axis=1)


def scan_body(count, heads, sent_ref, out_ref):
    keeps = sent_ref[:, heads, :].astype(F32) + sent_ref[:, heads + 1, :].astype(F32)
    keeps = keeps.T
    rows = sent_ref.shape[1]
    carried = jnp.zeros((rows, keeps.shape[0]), F32)
    for k in range(count):
        out_ref[k] = carried.astype(BF16)
        keep = keeps[:rows, k : k + 1]
        carried = keep * carried + sent_ref[k].astype(F32)


def scan_states(sent, heads):
    count = sent.shape[0]
    return pl.pallas_call(
        lambda sent_ref, out_ref: scan_body(count, heads, sent_ref, out_ref),
        out_shape=jax.ShapeDtypeStruct(sent.shape, BF16),
        in_specs=[pl.BlockSpec(memory_space=pltpu.VMEM)],
        out_specs=pl.BlockSpec(memory_space=pltpu.VMEM),
        cost_estimate=pl.CostEstimate(
            flops=2 * sent.size, bytes_accessed=4 * sent.size, transcendentals=0
        ),
    )(sent)


def pack_body(value_ref, shared_ref, step_ref, out_ref):
    inner, half, heads = value_ref.shape[1], shared_ref.shape[1] // 2, step_ref.shape[0]
    rest = out_ref.shape[2] - inner - half
    step = jnp.pad(step_ref[...].T, ((0, 0), (0, rest - heads)))
    packed = jnp.concatenate([value_ref[...], shared_ref[:, :half], step], axis=1).astype(BF16)
    for k in range(out_ref.shape[0]):
        out_ref[k] = packed


def pack_early(value, shared, step, copies):
    rows, inner = value.shape
    width = inner + shared.shape[1] // 2 + step.shape[1]
    width += -width % 128
    return pl.pallas_call(
        pack_body,
        out_shape=jax.ShapeDtypeStruct((copies, rows, width), BF16),
        in_specs=[pl.BlockSpec(memory_space=pltpu.VMEM)] * 3,
        out_specs=pl.BlockSpec(memory_space=pltpu.VMEM),
    )(value, shared, step.T)


def on_device(
    hidden_in,
    w_in_gate,
    w_in_value,
    w_in_shared,
    w_in_step,
    conv_value,
    conv_shared,
    dt_bias,
    a_log,
    skip_gain,
    norm_gain,
    w_out,
    prompt_lengths,
    row_blocks,
):
    x_size, z_size, core_size = SIZES
    seq_count = x_size * z_size * core_size
    tp_count = lax.axis_size("tp")
    tokens, features = hidden_in.shape
    rows_here, inner = w_in_value.shape
    shared = w_in_shared.shape[1]
    heads = dt_bias.shape[0]
    head_dim = inner // heads
    state = shared // 2
    x_at, z_at, core_at = (lax.axis_index(name) for name in SEQ)
    tp_at = lax.axis_index("tp")
    seq_at = (x_at * z_size + z_at) * core_size + core_at

    early = pack_early(w_in_value, w_in_shared, w_in_step, x_size * z_size)
    own = lax.all_to_all(early, SEQ[:2], 0, 0, tiled=True).reshape(-1, early.shape[2])

    late = jnp.concatenate(
        [w_in_gate.astype(BF16), w_out.T.astype(BF16), w_in_shared[:, state:].astype(BF16)], axis=1
    )
    late = lax.all_gather(late, SEQ, axis=0, tiled=True)

    before = lax.ppermute(
        hidden_in[tokens - EDGE :], SEQ, [(i, i + 1) for i in range(seq_count - 1)]
    )
    mine = jnp.concatenate([before, hidden_in], axis=0)
    hidden = jnp.concatenate([mine] + [ahead(mine, "tp", d) for d in range(1, tp_count)], axis=1)

    chips = jnp.arange(x_size * z_size, dtype=jnp.int32) * core_size
    blocks_each = seq_count // tp_count

    def columns_for(stored):
        model = jnp.take(row_blocks, stored)
        piece = (tp_at - model // blocks_each) % tp_count
        place = piece * blocks_each + model % blocks_each
        cut = hidden.reshape(hidden.shape[0], seq_count, rows_here)
        return jnp.take(cut, place, axis=1).reshape(hidden.shape[0], -1)

    h_all = columns_for(jnp.arange(seq_count, dtype=jnp.int32))
    h_own = columns_for(chips + core_at)
    h_other = columns_for(chips + (1 - core_at))
    own, h_own, h_other = lax.optimization_barrier((own, h_own, h_other))
    other = ahead(own, "core", 1)
    projected = (
        jnp.dot(h_own, own, preferred_element_type=F32)
        + jnp.dot(h_other, other, preferred_element_type=F32)
    ).astype(BF16)
    mixed = projected[:, : inner + state]
    raw = projected[EDGE:, inner + state : inner + state + heads]

    doc_ends = jnp.cumsum(prompt_lengths)
    first = seq_at * tokens
    ext_segments = segment_of(first - EDGE + jnp.arange(EDGE + tokens, dtype=jnp.int32), doc_ends)
    segments = ext_segments[EDGE:]
    prev_seg = ext_segments[EDGE - 1]

    def convolve(rows, taps):
        conv_sum = jnp.zeros((tokens, rows.shape[1]), F32)
        width = taps.shape[0]
        for k in range(width):
            at = EDGE - width + 1 + k
            same = (ext_segments[at : at + tokens] == segments)[:, None]
            conv_sum = conv_sum + jnp.where(
                same, taps[k][None, :] * rows[at : at + tokens].astype(F32), 0.0
            )
        return jax.nn.silu(conv_sum).astype(BF16)

    convolved = convolve(mixed, jnp.concatenate([conv_value, conv_shared[:, :state]], axis=1))
    values = convolved[:, :inner].reshape(tokens, heads, head_dim)
    b_half = convolved[:, inner:]
    steps = jax.nn.softplus(raw.astype(F32) + dt_bias[None, :])
    cumulative = jnp.cumsum(-steps * jnp.exp(a_log)[None, :], axis=0)

    tail = (
        jnp.where(
            (segments == segments[-1])[:, None], jnp.exp(cumulative[-1][None, :] - cumulative), 0.0
        )
        * steps
    )
    weighted = (tail[:, :, None] * values.astype(F32)).astype(BF16)
    fresh = lax.dot_general(
        weighted.reshape(tokens, inner), b_half, (((0,), (0,)), ((), ())), preferred_element_type=F32
    )
    keep = jnp.where(segments[-1] == prev_seg, jnp.exp(cumulative[-1]), 0.0)
    keep_hi = keep.astype(BF16)
    keep_lo = (keep - keep_hi.astype(F32)).astype(BF16)
    keep_rows = jnp.pad(jnp.stack([keep_hi, keep_lo]), ((0, 2), (0, state - heads)))
    sent = jnp.concatenate(
        [
            fresh.astype(BF16).reshape(heads, head_dim, state).transpose(1, 0, 2),
            jnp.broadcast_to(keep_rows[None], (head_dim,) + keep_rows.shape),
        ],
        axis=1,
    )
    received = lax.all_to_all(sent, SEQ, 0, 0, tiled=True)
    carried = lax.all_to_all(scan_states(received, heads), SEQ, 0, 0, tiled=True)
    carried = carried[:, :heads].transpose(1, 0, 2).reshape(inner, state)

    c_rows = jnp.dot(h_all, late[:, 2 * inner :], preferred_element_type=F32).astype(BF16)
    c_half = convolve(c_rows, conv_shared[:, state:])
    places = jnp.arange(tokens)
    causal = (places[:, None] >= places[None, :]) & (segments[:, None] == segments[None, :])
    scores = jnp.dot(c_half, b_half.T, preferred_element_type=F32)
    cum_t = cumulative.T
    gaps = jnp.where(causal[None], cum_t[:, :, None] - cum_t[:, None, :], -jnp.inf)
    weights = (scores[None] * jnp.exp(gaps) * steps.T[:, None, :]).astype(BF16)
    intra = jnp.einsum("hij,jhp->ihp", weights, values, preferred_element_type=F32)
    direct = intra + skip_gain[None, :, None] * values.astype(F32)
    carry_in = jnp.where((segments == prev_seg)[:, None], jnp.exp(cumulative), 0.0)

    gate = jnp.dot(h_all[EDGE:], late[:, :inner], preferred_element_type=F32).astype(BF16)
    inter = lax.dot_general(
        c_half, carried, (((1,), (1,)), ((), ())), preferred_element_type=F32
    ).reshape(tokens, heads, head_dim)
    mixed_heads = (direct + inter * carry_in[:, :, None]).reshape(tokens, inner)
    gated = mixed_heads * jax.nn.silu(gate.astype(F32))

    squares = lax.dot_general(
        jnp.ones((1, inner), F32),
        gated * gated,
        (((1,), (1,)), ((), ())),
        precision=lax.Precision.HIGHEST,
        preferred_element_type=F32,
    )
    squares_hi = squares.astype(BF16)
    squares_lo = (squares - squares_hi.astype(F32)).astype(BF16)
    riding = jnp.concatenate([squares_hi, squares_lo], axis=0)
    riding = jnp.pad(riding, ((0, 6), (0, features - tokens)))
    terms = lax.dot_general(
        (gated * norm_gain[None, :]).astype(BF16),
        late[:, inner : 2 * inner],
        (((1,), (1,)), ((), ())),
        preferred_element_type=F32,
    ).astype(BF16)

    def share(d):
        cut = lax.dynamic_slice_in_dim(terms, ((tp_at + d) % tp_count) * features, features, 1)
        return jnp.concatenate([cut, riding], axis=0)

    parts = [share(0)] + [ahead(share(d), "tp", d) for d in range(1, tp_count)]
    summed = sum(part.astype(F32) for part in parts)
    total = summed[tokens, :tokens] + summed[tokens + 1, :tokens]
    scale = lax.rsqrt(total / (inner * tp_count) + EPSILON)
    return (summed[:tokens] * scale[:, None]).astype(BF16)


def solution(mesh):
    fine = Mesh(mesh.devices.reshape(SIZES + (-1,)), SEQ + ("tp",))
    return jax.shard_map(
        on_device,
        mesh=fine,
        in_specs=(
            P(SEQ, "tp"),
            P(SEQ, "tp"),
            P(SEQ, "tp"),
            P(SEQ, None),
            P(SEQ, "tp"),
            P(None, "tp"),
            P(),
            P("tp"),
            P("tp"),
            P("tp"),
            P("tp"),
            P("tp", SEQ),
            P(),
            P(),
        ),
        out_specs=P(SEQ, "tp"),
        check_vma=False,
    )
```

```python
import jax
import jax.numpy as jnp
from jax import lax
from jax.experimental import pallas as pl
from jax.experimental.pallas import tpu as pltpu
from jax.sharding import Mesh, PartitionSpec as P

EPSILON = 1e-05
EDGE = 8
SEQ = ("x", "z", "core")
SIZES = (4, 8, 2)
BF16 = jnp.bfloat16
F32 = jnp.float32


def ahead(block, axis, distance):
    count = lax.axis_size(axis)
    return lax.ppermute(block, axis, [(i, (i + distance) % count) for i in range(count)])


def segment_of(positions, doc_ends):
    return jnp.sum((positions[:, None] >= doc_ends[None, :]).astype(jnp.int32), axis=1)


def scan_body(count, heads, sent_ref, out_ref):
    keeps = sent_ref[:, heads, :].astype(F32) + sent_ref[:, heads + 1, :].astype(F32)
    keeps = keeps.T
    rows = sent_ref.shape[1]
    carried = jnp.zeros((rows, keeps.shape[0]), F32)
    for k in range(count):
        out_ref[k] = carried.astype(BF16)
        keep = keeps[:rows, k : k + 1]
        carried = keep * carried + sent_ref[k].astype(F32)


def scan_states(sent, heads):
    count = sent.shape[0]
    return pl.pallas_call(
        lambda sent_ref, out_ref: scan_body(count, heads, sent_ref, out_ref),
        out_shape=jax.ShapeDtypeStruct(sent.shape, BF16),
        in_specs=[pl.BlockSpec(memory_space=pltpu.VMEM)],
        out_specs=pl.BlockSpec(memory_space=pltpu.VMEM),
        cost_estimate=pl.CostEstimate(
            flops=2 * sent.size, bytes_accessed=4 * sent.size, transcendentals=0
        ),
    )(sent)


def pack_body(value_ref, shared_ref, step_ref, out_ref):
    inner, half, heads = value_ref.shape[1], shared_ref.shape[1] // 2, step_ref.shape[0]
    rest = out_ref.shape[1] - inner - half
    step = jnp.pad(step_ref[...].T, ((0, 0), (0, rest - heads)))
    out_ref[:, :inner] = value_ref[...].astype(BF16)
    out_ref[:, inner : inner + half] = shared_ref[:, :half].astype(BF16)
    out_ref[:, inner + half :] = step.astype(BF16)


def pack_early(value, shared, step):
    rows, inner = value.shape
    width = inner + shared.shape[1] // 2 + step.shape[1]
    width += -width % 128
    return pl.pallas_call(
        pack_body,
        out_shape=jax.ShapeDtypeStruct((rows, width), BF16),
        in_specs=[pl.BlockSpec(memory_space=pltpu.VMEM)] * 3,
        out_specs=pl.BlockSpec(memory_space=pltpu.VMEM),
    )(value, shared, step.T)


def project_body(h_ref, *refs):
    *blocks, out_ref, held = refs
    depth = blocks[0].shape[0]
    for i, block in enumerate(blocks):
        held[i * depth : (i + 1) * depth] = block[...]
    width = 256
    for at in range(0, out_ref.shape[1], width):
        end = min(at + width, out_ref.shape[1])
        out_ref[:, at:end] = jnp.dot(
            h_ref[...], held[:, at:end], preferred_element_type=F32
        ).astype(BF16)


def project(h, blocks):
    depth, width = blocks[0].shape
    rows, features = h.shape
    return pl.pallas_call(
        project_body,
        out_shape=jax.ShapeDtypeStruct((rows, width), BF16),
        in_specs=[pl.BlockSpec(memory_space=pltpu.VMEM)] * (1 + len(blocks)),
        out_specs=pl.BlockSpec(memory_space=pltpu.VMEM),
        scratch_shapes=[pltpu.VMEM((features, width), BF16)],
        compiler_params=pltpu.CompilerParams(vmem_limit_bytes=32 << 20),
        cost_estimate=pl.CostEstimate(
            flops=2 * rows * features * width, bytes_accessed=2 * features * width, transcendentals=0
        ),
    )(h, *blocks)


def on_device(
    hidden_in,
    w_in_gate,
    w_in_value,
    w_in_shared,
    w_in_step,
    conv_value,
    conv_shared,
    dt_bias,
    a_log,
    skip_gain,
    norm_gain,
    w_out,
    prompt_lengths,
    row_blocks,
):
    x_size, z_size, core_size = SIZES
    seq_count = x_size * z_size * core_size
    tp_count = lax.axis_size("tp")
    tokens, features = hidden_in.shape
    rows_here, inner = w_in_value.shape
    shared = w_in_shared.shape[1]
    heads = dt_bias.shape[0]
    head_dim = inner // heads
    state = shared // 2
    x_at, z_at, core_at = (lax.axis_index(name) for name in SEQ)
    tp_at = lax.axis_index("tp")
    seq_at = (x_at * z_size + z_at) * core_size + core_at

    half = z_size // 2
    z_shifts = [1, 2, z_size - 1]
    z_offsets = [(d + o) % z_size for d in [0] + z_shifts for o in (0, half)]
    x_shifts = list(range(1, x_size))

    def z_pair(block):
        return jnp.concatenate([block, ahead(block, "z", half)], axis=0)

    def z_all(pair):
        return jnp.concatenate([pair] + [ahead(pair, "z", d) for d in z_shifts], axis=0)

    def x_all(block):
        return [block] + [ahead(block, "x", d) for d in x_shifts]

    tie = lax.optimization_barrier

    early = pack_early(w_in_value, w_in_shared, w_in_step)
    before = lax.ppermute(
        hidden_in[tokens - EDGE :], SEQ, [(i, i + 1) for i in range(seq_count - 1)]
    )
    along_z = z_all(z_pair(early))
    late = jnp.concatenate(
        [w_in_gate.astype(BF16), w_in_shared[:, state:].astype(BF16), w_out.T.astype(BF16)], axis=1
    )
    late_pair = z_pair(late)
    mine = jnp.concatenate([before, hidden_in], axis=0)
    next_to = [ahead(mine, "tp", d) for d in (1, tp_count - 1)]
    along_z, next_to, late_pair = tie((along_z, next_to, late_pair))
    own = x_all(along_z)
    across = [ahead(mine, "tp", d) for d in range(2, tp_count - 1)]
    hidden = jnp.concatenate([mine, next_to[0]] + across + [next_to[1]], axis=1)

    chips = jnp.concatenate(
        [
            jnp.stack([((x_at - d) % x_size * z_size + (z_at - o) % z_size) for o in z_offsets])
            for d in range(x_size)
        ]
    )
    stored = jnp.concatenate([chips * core_size + core_at, chips * core_size + 1 - core_at])
    blocks_each = seq_count // tp_count
    model = jnp.take(row_blocks, stored)
    place = (tp_at - model // blocks_each) % tp_count * blocks_each + model % blocks_each
    h = jnp.take(hidden.reshape(hidden.shape[0], seq_count, rows_here), place, axis=1)
    h = h.reshape(hidden.shape[0], -1)
    own[-1], h = tie((own[-1], h))
    other = [ahead(block, "core", 1) for block in own]
    late_pair, own[-1] = tie((late_pair, own[-1]))
    late_z = z_all(late_pair)
    projected = project(h, own + other)
    mixed = projected[:, : inner + state]
    raw = projected[EDGE:, inner + state : inner + state + heads]

    doc_ends = jnp.cumsum(prompt_lengths)
    first = seq_at * tokens
    ext_segments = segment_of(first - EDGE + jnp.arange(EDGE + tokens, dtype=jnp.int32), doc_ends)
    segments = ext_segments[EDGE:]
    prev_seg = ext_segments[EDGE - 1]

    def convolve(rows, taps):
        conv_sum = jnp.zeros((tokens, rows.shape[1]), F32)
        width = taps.shape[0]
        for k in range(width):
            at = EDGE - width + 1 + k
            same = (ext_segments[at : at + tokens] == segments)[:, None]
            conv_sum = conv_sum + jnp.where(
                same, taps[k][None, :] * rows[at : at + tokens].astype(F32), 0.0
            )
        return jax.nn.silu(conv_sum).astype(BF16)

    convolved = convolve(mixed, jnp.concatenate([conv_value, conv_shared[:, :state]], axis=1))
    values = convolved[:, :inner].reshape(tokens, heads, head_dim)
    b_half = convolved[:, inner:]
    steps = jax.nn.softplus(raw.astype(F32) + dt_bias[None, :])
    cumulative = jnp.cumsum(-steps * jnp.exp(a_log)[None, :], axis=0)

    tail = (
        jnp.where(
            (segments == segments[-1])[:, None], jnp.exp(cumulative[-1][None, :] - cumulative), 0.0
        )
        * steps
    )
    weighted = (tail[:, :, None] * values.astype(F32)).astype(BF16)
    fresh = lax.dot_general(
        weighted.reshape(tokens, inner), b_half, (((0,), (0,)), ((), ())), preferred_element_type=F32
    )
    keep = jnp.where(segments[-1] == prev_seg, jnp.exp(cumulative[-1]), 0.0)
    keep_hi = keep.astype(BF16)
    keep_lo = (keep - keep_hi.astype(F32)).astype(BF16)
    keep_rows = jnp.pad(jnp.stack([keep_hi, keep_lo]), ((0, 2), (0, state - heads)))
    sent = jnp.concatenate(
        [
            fresh.astype(BF16).reshape(heads, head_dim, state).transpose(1, 0, 2),
            jnp.broadcast_to(keep_rows[None], (head_dim,) + keep_rows.shape),
        ],
        axis=1,
    )
    sent, late_z = tie((sent, late_z))
    received = lax.all_to_all(sent, SEQ, 0, 0, tiled=True)
    gate_own = x_all(late_z[:, : inner + state])
    received, gate_own = tie((received, gate_own))
    carried = lax.all_to_all(scan_states(received, heads), SEQ, 0, 0, tiled=True)
    gate_other = [ahead(block, "core", 1) for block in gate_own]
    gate_all = project(h, gate_own + gate_other)
    out_own = x_all(late_z[:, inner + state :])
    carried, out_own = tie((carried, out_own))
    out_other = [ahead(block, "core", 1) for block in out_own]
    carried = carried[:, :heads].transpose(1, 0, 2).reshape(inner, state)

    c_half = convolve(gate_all[:, inner:], conv_shared[:, state:])
    places = jnp.arange(tokens)
    causal = (places[:, None] >= places[None, :]) & (segments[:, None] == segments[None, :])
    scores = jnp.dot(c_half, b_half.T, preferred_element_type=F32)
    cum_t = cumulative.T
    gaps = jnp.where(causal[None], cum_t[:, :, None] - cum_t[:, None, :], -jnp.inf)
    weights = (scores[None] * jnp.exp(gaps) * steps.T[:, None, :]).astype(BF16)
    intra = jnp.einsum("hij,jhp->ihp", weights, values, preferred_element_type=F32)
    direct = intra + skip_gain[None, :, None] * values.astype(F32)
    carry_in = jnp.where((segments == prev_seg)[:, None], jnp.exp(cumulative), 0.0)

    gate = gate_all[EDGE:, :inner]
    inter = lax.dot_general(
        c_half, carried, (((1,), (1,)), ((), ())), preferred_element_type=F32
    ).reshape(tokens, heads, head_dim)
    mixed_heads = (direct + inter * carry_in[:, :, None]).reshape(tokens, inner)
    gated = mixed_heads * jax.nn.silu(gate.astype(F32))

    squares = lax.dot_general(
        jnp.ones((1, inner), F32),
        gated * gated,
        (((1,), (1,)), ((), ())),
        precision=lax.Precision.HIGHEST,
        preferred_element_type=F32,
    )
    squares_hi = squares.astype(BF16)
    squares_lo = (squares - squares_hi.astype(F32)).astype(BF16)
    riding = jnp.concatenate([squares_hi, squares_lo], axis=0)
    riding = jnp.pad(riding, ((0, 6), (0, features - tokens)))
    normed = (gated * norm_gain[None, :]).astype(BF16)
    terms = jnp.stack(
        [
            lax.dot_general(
                normed,
                jnp.concatenate(pair, axis=0),
                (((1,), (1,)), ((), ())),
                preferred_element_type=F32,
            ).astype(BF16)
            for pair in zip(out_own, out_other)
        ]
    )

    def share(d):
        cut = lax.dynamic_index_in_dim(terms, (x_at - tp_at - d) % x_size, 0, keepdims=False)
        return jnp.concatenate([cut, riding], axis=0)

    parts = [share(0)] + [ahead(share(d), "tp", d) for d in range(1, tp_count)]
    summed = sum(part.astype(F32) for part in parts)
    total = summed[tokens, :tokens] + summed[tokens + 1, :tokens]
    scale = lax.rsqrt(total / (inner * tp_count) + EPSILON)
    result = (summed[:tokens] * scale[:, None]).astype(BF16)

    lane = jnp.arange(features, dtype=jnp.int32)
    part, rest = lane // (z_size * rows_here), lane % (z_size * rows_here)
    offset = jnp.take(jnp.array(z_offsets, jnp.int32), rest // rows_here)
    core_of = jnp.where(part == 0, core_at, 1 - core_at)
    target = ((z_at - offset) % z_size * core_size + core_of) * rows_here + rest % rows_here
    moves = (target[:, None] == lane[None, :]).astype(BF16)
    return jnp.dot(result, moves, preferred_element_type=F32).astype(BF16)


def solution(mesh):
    fine = Mesh(mesh.devices.reshape(SIZES + (-1,)), SEQ + ("tp",))
    return jax.shard_map(
        on_device,
        mesh=fine,
        in_specs=(
            P(SEQ, "tp"),
            P(SEQ, "tp"),
            P(SEQ, "tp"),
            P(SEQ, None),
            P(SEQ, "tp"),
            P(None, "tp"),
            P(),
            P("tp"),
            P("tp"),
            P("tp"),
            P("tp"),
            P("tp", SEQ),
            P(),
            P(),
        ),
        out_specs=P(SEQ, "tp"),
        check_vma=False,
    )
```

```python
import jax
import jax.numpy as jnp
from jax import lax
from jax.experimental import pallas as pl
from jax.experimental.pallas import tpu as pltpu
from jax.sharding import Mesh, PartitionSpec as P

EPSILON = 1e-05
EDGE = 8
SEQ = ("x", "z", "core")
SIZES = (4, 8, 2)
BF16 = jnp.bfloat16
F32 = jnp.float32


def ahead(block, axis, distance):
    count = lax.axis_size(axis)
    return lax.ppermute(block, axis, [(i, (i + distance) % count) for i in range(count)])


def segment_of(positions, doc_ends):
    return jnp.sum((positions[:, None] >= doc_ends[None, :]).astype(jnp.int32), axis=1)


def scan_body(count, heads, sent_ref, out_ref):
    keeps = sent_ref[:, heads, :].astype(F32) + sent_ref[:, heads + 1, :].astype(F32)
    keeps = keeps.T
    rows = sent_ref.shape[1]
    carried = jnp.zeros((rows, keeps.shape[0]), F32)
    for k in range(count):
        out_ref[k] = carried.astype(BF16)
        keep = keeps[:rows, k : k + 1]
        carried = keep * carried + sent_ref[k].astype(F32)


def scan_states(sent, heads):
    count = sent.shape[0]
    return pl.pallas_call(
        lambda sent_ref, out_ref: scan_body(count, heads, sent_ref, out_ref),
        out_shape=jax.ShapeDtypeStruct(sent.shape, BF16),
        in_specs=[pl.BlockSpec(memory_space=pltpu.VMEM)],
        out_specs=pl.BlockSpec(memory_space=pltpu.VMEM),
        cost_estimate=pl.CostEstimate(
            flops=2 * sent.size, bytes_accessed=4 * sent.size, transcendentals=0
        ),
    )(sent)


def pack_body(value_ref, shared_ref, step_ref, gate_ref, out_t_ref, out_ref):
    inner, half, heads = value_ref.shape[1], shared_ref.shape[1] // 2, step_ref.shape[0]
    rest = -heads % 128
    step = jnp.pad(step_ref[...].T, ((0, 0), (0, rest)))
    at = 0
    for piece in (
        value_ref[...],
        shared_ref[:, :half],
        step,
        gate_ref[...],
        shared_ref[:, half:],
        out_t_ref[...],
    ):
        out_ref[:, at : at + piece.shape[1]] = piece.astype(BF16)
        at += piece.shape[1]


def pack(value, shared, step, gate, out_t):
    rows, inner = value.shape
    heads = step.shape[1]
    width = 3 * inner + shared.shape[1] + heads + -heads % 128
    return pl.pallas_call(
        pack_body,
        out_shape=jax.ShapeDtypeStruct((rows, width), BF16),
        in_specs=[pl.BlockSpec(memory_space=pltpu.VMEM)] * 5,
        out_specs=pl.BlockSpec(memory_space=pltpu.VMEM),
    )(value, shared, step.T, gate, out_t)


def project_body(h_ref, *refs):
    *blocks, out_ref, held = refs
    depth = blocks[0].shape[0]
    for i, block in enumerate(blocks):
        held[i * depth : (i + 1) * depth] = block[:, : held.shape[1]]
    width = 256
    for at in range(0, out_ref.shape[1], width):
        end = min(at + width, out_ref.shape[1])
        out_ref[:, at:end] = jnp.dot(
            h_ref[...], held[:, at:end], preferred_element_type=F32
        ).astype(BF16)


def project(h, blocks, width):
    rows, features = h.shape
    return pl.pallas_call(
        project_body,
        out_shape=jax.ShapeDtypeStruct((rows, width), BF16),
        in_specs=[pl.BlockSpec(memory_space=pltpu.VMEM)] * (1 + len(blocks)),
        out_specs=pl.BlockSpec(memory_space=pltpu.VMEM),
        scratch_shapes=[pltpu.VMEM((features, width), BF16)],
        compiler_params=pltpu.CompilerParams(vmem_limit_bytes=32 << 20),
        cost_estimate=pl.CostEstimate(
            flops=2 * rows * features * width, bytes_accessed=2 * features * width, transcendentals=0
        ),
    )(h, *blocks)


def on_device(
    hidden_in,
    w_in_gate,
    w_in_value,
    w_in_shared,
    w_in_step,
    conv_value,
    conv_shared,
    dt_bias,
    a_log,
    skip_gain,
    norm_gain,
    w_out,
    prompt_lengths,
    row_blocks,
):
    x_size, z_size, core_size = SIZES
    seq_count = x_size * z_size * core_size
    tp_count = lax.axis_size("tp")
    tokens, features = hidden_in.shape
    rows_here, inner = w_in_value.shape
    shared = w_in_shared.shape[1]
    heads = dt_bias.shape[0]
    head_dim = inner // heads
    state = shared // 2
    x_at, z_at, core_at = (lax.axis_index(name) for name in SEQ)
    tp_at = lax.axis_index("tp")
    seq_at = (x_at * z_size + z_at) * core_size + core_at

    x_shifts = list(range(1, x_size))

    def x_all(block):
        return [block] + [ahead(block, "x", d) for d in x_shifts]

    tie = lax.optimization_barrier

    before = lax.ppermute(
        hidden_in[tokens - EDGE :], SEQ, [(i, i + 1) for i in range(seq_count - 1)]
    )
    packed = pack(w_in_value, w_in_shared, w_in_step, w_in_gate, w_out.T)
    packed, before = tie((packed, before))
    along_z = lax.all_gather(packed, "z", axis=0, tiled=True)
    early_width = packed.shape[1] - 2 * inner - state
    own = x_all(along_z[:, :early_width])
    late = along_z[:, early_width:]
    mine = jnp.concatenate([before, hidden_in], axis=0)
    hidden = jnp.concatenate([mine] + [ahead(mine, "tp", d) for d in range(1, tp_count)], axis=1)

    chips = jnp.concatenate(
        [
            (x_at - d) % x_size * z_size + jnp.arange(z_size, dtype=jnp.int32)
            for d in range(x_size)
        ]
    )
    stored = jnp.concatenate([chips * core_size + core_at, chips * core_size + 1 - core_at])
    blocks_each = seq_count // tp_count
    model = jnp.take(row_blocks, stored)
    place = (tp_at - model // blocks_each) % tp_count * blocks_each + model % blocks_each
    h = jnp.take(hidden.reshape(hidden.shape[0], seq_count, rows_here), place, axis=1)
    h = h.reshape(hidden.shape[0], -1)
    own[-1], h, late = tie((own[-1], h, late))
    other = [ahead(block, "core", 1) for block in own]
    late_own = x_all(late)
    projected = project(h, own + other, early_width)
    mixed = projected[:, : inner + state]
    raw = projected[EDGE:, inner + state : inner + state + heads]

    doc_ends = jnp.cumsum(prompt_lengths)
    first = seq_at * tokens
    ext_segments = segment_of(first - EDGE + jnp.arange(EDGE + tokens, dtype=jnp.int32), doc_ends)
    segments = ext_segments[EDGE:]
    prev_seg = ext_segments[EDGE - 1]

    def convolve(rows, taps):
        conv_sum = jnp.zeros((tokens, rows.shape[1]), F32)
        width = taps.shape[0]
        for k in range(width):
            at = EDGE - width + 1 + k
            same = (ext_segments[at : at + tokens] == segments)[:, None]
            conv_sum = conv_sum + jnp.where(
                same, taps[k][None, :] * rows[at : at + tokens].astype(F32), 0.0
            )
        return jax.nn.silu(conv_sum).astype(BF16)

    convolved = convolve(mixed, jnp.concatenate([conv_value, conv_shared[:, :state]], axis=1))
    values = convolved[:, :inner].reshape(tokens, heads, head_dim)
    b_half = convolved[:, inner:]
    steps = jax.nn.softplus(raw.astype(F32) + dt_bias[None, :])
    cumulative = jnp.cumsum(-steps * jnp.exp(a_log)[None, :], axis=0)

    tail = (
        jnp.where(
            (segments == segments[-1])[:, None], jnp.exp(cumulative[-1][None, :] - cumulative), 0.0
        )
        * steps
    )
    weighted = (tail[:, :, None] * values.astype(F32)).astype(BF16)
    fresh = lax.dot_general(
        weighted.reshape(tokens, inner), b_half, (((0,), (0,)), ((), ())), preferred_element_type=F32
    )
    keep = jnp.where(segments[-1] == prev_seg, jnp.exp(cumulative[-1]), 0.0)
    keep_hi = keep.astype(BF16)
    keep_lo = (keep - keep_hi.astype(F32)).astype(BF16)
    keep_rows = jnp.pad(jnp.stack([keep_hi, keep_lo]), ((0, 2), (0, state - heads)))
    sent = jnp.concatenate(
        [
            fresh.astype(BF16).reshape(heads, head_dim, state).transpose(1, 0, 2),
            jnp.broadcast_to(keep_rows[None], (head_dim,) + keep_rows.shape),
        ],
        axis=1,
    )
    received = lax.all_to_all(sent, SEQ, 0, 0, tiled=True)
    received, late_own = tie((received, late_own))
    carried = lax.all_to_all(scan_states(received, heads), SEQ, 0, 0, tiled=True)
    late_other = [ahead(block, "core", 1) for block in late_own]
    gate_all = project(h, late_own + late_other, inner + state)
    out_own = [block[:, inner + state :] for block in late_own]
    out_other = [block[:, inner + state :] for block in late_other]
    carried = carried[:, :heads].transpose(1, 0, 2).reshape(inner, state)

    c_half = convolve(gate_all[:, inner:], conv_shared[:, state:])
    places = jnp.arange(tokens)
    causal = (places[:, None] >= places[None, :]) & (segments[:, None] == segments[None, :])
    scores = jnp.dot(c_half, b_half.T, preferred_element_type=F32)
    cum_t = cumulative.T
    gaps = jnp.where(causal[None], cum_t[:, :, None] - cum_t[:, None, :], -jnp.inf)
    weights = (scores[None] * jnp.exp(gaps) * steps.T[:, None, :]).astype(BF16)
    intra = jnp.einsum("hij,jhp->ihp", weights, values, preferred_element_type=F32)
    direct = intra + skip_gain[None, :, None] * values.astype(F32)
    carry_in = jnp.where((segments == prev_seg)[:, None], jnp.exp(cumulative), 0.0)

    gate = gate_all[EDGE:, :inner]
    inter = lax.dot_general(
        c_half, carried, (((1,), (1,)), ((), ())), preferred_element_type=F32
    ).reshape(tokens, heads, head_dim)
    mixed_heads = (direct + inter * carry_in[:, :, None]).reshape(tokens, inner)
    gated = mixed_heads * jax.nn.silu(gate.astype(F32))

    squares = lax.dot_general(
        jnp.ones((1, inner), F32),
        gated * gated,
        (((1,), (1,)), ((), ())),
        precision=lax.Precision.HIGHEST,
        preferred_element_type=F32,
    )
    squares_hi = squares.astype(BF16)
    squares_lo = (squares - squares_hi.astype(F32)).astype(BF16)
    riding = jnp.concatenate([squares_hi, squares_lo], axis=0)
    riding = jnp.pad(riding, ((0, 6), (0, features - tokens)))
    normed = (gated * norm_gain[None, :]).astype(BF16)
    terms = jnp.stack(
        [
            lax.dot_general(
                normed,
                jnp.concatenate(pair, axis=0),
                (((1,), (1,)), ((), ())),
                preferred_element_type=F32,
            ).astype(BF16)
            for pair in zip(out_own, out_other)
        ]
    )

    def share(d):
        cut = lax.dynamic_index_in_dim(terms, (x_at - tp_at - d) % x_size, 0, keepdims=False)
        return jnp.concatenate([cut, riding], axis=0)

    parts = [share(0)] + [ahead(share(d), "tp", d) for d in range(1, tp_count)]
    summed = sum(part.astype(F32) for part in parts)
    total = summed[tokens, :tokens] + summed[tokens + 1, :tokens]
    scale = lax.rsqrt(total / (inner * tp_count) + EPSILON)
    result = (summed[:tokens] * scale[:, None]).astype(BF16)

    lane = jnp.arange(features, dtype=jnp.int32)
    part, rest = lane // (z_size * rows_here), lane % (z_size * rows_here)
    core_of = jnp.where(part == 0, core_at, 1 - core_at)
    target = (rest // rows_here * core_size + core_of) * rows_here + rest % rows_here
    moves = (target[:, None] == lane[None, :]).astype(BF16)
    return jnp.dot(result, moves, preferred_element_type=F32).astype(BF16)


def solution(mesh):
    fine = Mesh(mesh.devices.reshape(SIZES + (-1,)), SEQ + ("tp",))
    return jax.shard_map(
        on_device,
        mesh=fine,
        in_specs=(
            P(SEQ, "tp"),
            P(SEQ, "tp"),
            P(SEQ, "tp"),
            P(SEQ, None),
            P(SEQ, "tp"),
            P(None, "tp"),
            P(),
            P("tp"),
            P("tp"),
            P("tp"),
            P("tp"),
            P("tp", SEQ),
            P(),
            P(),
        ),
        out_specs=P(SEQ, "tp"),
        check_vma=False,
    )
```

```python
import functools

import jax
import jax.numpy as jnp
from jax import lax
from jax.experimental import pallas as pl
from jax.experimental.pallas import tpu as pltpu
from jax.sharding import Mesh, PartitionSpec as P

EPSILON = 1e-05
EDGE = 8
LINES = 16
SEQ = ("x", "z", "core")
SIZES = (4, 8, 2)
BF16 = jnp.bfloat16
F32 = jnp.float32


def ahead(block, axis, distance):
    count = lax.axis_size(axis)
    return lax.ppermute(block, axis, [(i, (i + distance) % count) for i in range(count)])


def pack_body(value_ref, shared_ref, step_ref, gate_ref, out_t_ref, out_ref):
    inner, half, heads = value_ref.shape[1], shared_ref.shape[1] // 2, step_ref.shape[0]
    rest = -heads % 128
    step = jnp.pad(step_ref[...].T, ((0, 0), (0, rest)))
    at = 0
    for piece in (
        value_ref[...],
        shared_ref[:, :half],
        step,
        gate_ref[...],
        shared_ref[:, half:],
        out_t_ref[...],
    ):
        out_ref[:, at : at + piece.shape[1]] = piece.astype(BF16)
        at += piece.shape[1]


def pack(value, shared, step, gate, out_t):
    rows, inner = value.shape
    heads = step.shape[1]
    width = 3 * inner + shared.shape[1] + heads + -heads % 128
    return pl.pallas_call(
        pack_body,
        out_shape=jax.ShapeDtypeStruct((rows, width), BF16),
        in_specs=[pl.BlockSpec(memory_space=pltpu.VMEM)] * 5,
        out_specs=pl.BlockSpec(memory_space=pltpu.VMEM),
    )(value, shared, step.T, gate, out_t)


def call(body, shapes, args, scalars=0, scratch=(), flops=0):
    smem, vmem = pl.BlockSpec(memory_space=pltpu.SMEM), pl.BlockSpec(memory_space=pltpu.VMEM)
    moved = sum(x.size * x.dtype.itemsize for x in args)
    return pl.pallas_call(
        body,
        out_shape=[jax.ShapeDtypeStruct(shape, kind) for shape, kind in shapes],
        in_specs=[smem] * scalars + [vmem] * (len(args) - scalars),
        out_specs=[vmem] * len(shapes),
        scratch_shapes=[pltpu.VMEM(shape, kind) for shape, kind in scratch],
        compiler_params=pltpu.CompilerParams(vmem_limit_bytes=44 << 20),
        cost_estimate=pl.CostEstimate(flops=flops, bytes_accessed=moved, transcendentals=0),
    )(*args)


def dot(a, b, **kw):
    return jnp.dot(a, b, preferred_element_type=F32, **kw)


def iota(shape, dim):
    return lax.broadcasted_iota(jnp.int32, shape, dim)


def one_hot(rows, columns, width, wrap):
    return ((iota((rows, columns), 0) & (wrap - 1)) == iota((rows, columns), 1) // width).astype(BF16)


def spread(x, head_of):
    hi = x.astype(BF16)
    return dot(hi, head_of) + dot((x - hi.astype(F32)).astype(BF16), head_of)


def prompt_start(ends_ref, positions):
    start = jnp.zeros_like(positions)
    for i in range(ends_ref.shape[0]):
        start = jnp.maximum(start, jnp.where(positions >= ends_ref[i], ends_ref[i], 0))
    return start


def silu(x):
    return x / (1.0 + jnp.exp(-x))


def convolve(rows_ref, at, taps, positions, start):
    tokens, width = positions.shape[0], taps.shape[0]
    total = jnp.zeros(positions.shape, F32)
    for k in range(width):
        back = width - 1 - k
        rows = rows_ref[EDGE - back : EDGE - back + tokens, at : at + positions.shape[1]]
        total = total + jnp.where(positions - back >= start, taps[k : k + 1] * rows, 0.0)
    return silu(total).astype(BF16)


def gather_blocks(blocks, held):
    depth = blocks[0].shape[0]
    for i, block in enumerate(blocks):
        held[i * depth : (i + 1) * depth] = block[:, : held.shape[1]]


def early_body(head_dim, first_ref, ends_ref, h_ref, *refs):
    *blocks, conv_value, conv_shared, bias, a_log = refs[:-8]
    x_ref, b_ref, dt_ref, cum_ref, sent_ref, held, rows, lines = refs[-8:]
    tokens, inner = x_ref.shape
    gather_blocks(blocks, held)
    for at in range(0, held.shape[1], 256):
        rows[:, at : at + 256] = dot(h_ref[...], held[:, at : at + 256]).astype(BF16).astype(F32)
    first = first_ref[0]
    positions = first + iota((tokens, 128), 0)
    start = prompt_start(ends_ref, positions)
    last_start = prompt_start(ends_ref, first + tokens - 1)
    for at in range(0, inner, 128):
        x_ref[:, at : at + 128] = convolve(
            rows, at, conv_value[:, at : at + 128], positions, start
        )
    b_half = convolve(rows, inner, conv_shared[:, :128], positions, start)
    b_ref[...] = b_half
    raw = rows[EDGE:, inner + 128 :] + bias[...]
    dt = jnp.maximum(raw, 0.0) + jnp.log1p(jnp.exp(-jnp.abs(raw)))
    below = (iota((tokens, tokens), 0) >= iota((tokens, tokens), 1)).astype(F32)
    cum = dot(below, -dt * jnp.exp(a_log[...]), precision=lax.Precision.HIGHEST)
    dt_ref[...] = dt
    cum_ref[...] = cum
    last = cum[tokens - 1 :]
    tail = jnp.where(positions >= last_start, jnp.exp(last - cum), 0.0) * dt
    head_of = one_hot(128, inner, head_dim, 128)
    weighted = (spread(tail, head_of) * x_ref[...].astype(F32)).astype(BF16)
    fresh = dot(b_half.astype(F32).T.astype(BF16), weighted)
    lines[...] = jnp.zeros_like(lines)
    count = lines.shape[0] // LINES
    line = 0
    for row in range(0, fresh.shape[0], count):
        for at in range(0, inner, 128):
            lines[pl.ds(line, count, stride=LINES), :] = fresh[row : row + count, at : at + 128]
            line += 1
    keep = jnp.where(last_start < first, jnp.exp(last), 0.0)
    keep = jnp.broadcast_to(keep, (8, 128))
    keep_hi = keep.astype(BF16).astype(F32)
    keep_lo = pltpu.roll(keep - keep_hi, 64, axis=1)
    both = jnp.where(iota((8, 128), 1) < 64, keep_hi, keep_lo)
    lines[pl.ds(line, count, stride=LINES), :] = jnp.concatenate([both] * (count // 8), axis=0)
    sent_ref[...] = lines[...].astype(BF16)


def scan_body(head_dim, inner, copies, sent_ref, out_ref, lines):
    lines[...] = sent_ref[...].astype(F32)
    count = lines.shape[0] // LINES
    tiles = inner // 128

    def line(r):
        return lines[pl.ds(r, count, stride=LINES), :]

    keeps = line(copies * tiles).astype(BF16)
    row = iota((count, 128), 0)

    def down(x, d):
        return jnp.where(row >= d, pltpu.roll(x, d, axis=0), 0.0)

    head_of = one_hot(128, inner, head_dim, 64)
    for t in range(tiles):
        keep = dot(keeps, head_of[:, t * 128 : (t + 1) * 128])
        states = [line(i * tiles + t) for i in range(copies)]
        d = 1
        while d < count:
            states = [x + keep * down(x, d) for x in states]
            keep = keep * down(keep, d)
            d *= 2
        for i, x in enumerate(states):
            lines[pl.ds(i * tiles + t, count, stride=LINES), :] = down(x, 1)
    out_ref[...] = lines[...].astype(BF16)


def middle_body(head_dim, first_ref, ends_ref, h_ref, *refs):
    *blocks, conv_shared, x_ref, b_ref, dt_ref, cum_ref, skip = refs[:-7]
    direct_ref, carry_ref, c_ref, out_w_ref, held, c_rows, gate = refs[-7:]
    tokens, inner = x_ref.shape
    gather_blocks(blocks, held)
    wide = held.shape[1]
    half = len(blocks) // 2
    depth = blocks[0].shape[0]
    for i in range(half):
        for j, block in enumerate((blocks[i], blocks[half + i])):
            at = (2 * i + j) * depth
            out_w_ref[at : at + depth] = block[:, wide:]
    for at in range(0, inner, 256):
        g = dot(h_ref[EDGE:], held[:, at : at + 256])
        gate[:, at : at + 256] = silu(g.astype(BF16).astype(F32))
    c_rows[...] = dot(h_ref[...], held[:, inner:]).astype(BF16).astype(F32)
    first = first_ref[0]
    positions = first + iota((tokens, 128), 0)
    start = prompt_start(ends_ref, positions)
    c_half = convolve(c_rows, 0, conv_shared[:, 128:], positions, start)
    c_ref[...] = c_half
    scores = lax.dot_general(
        c_half, b_ref[...], (((1,), (1,)), ((), ())), preferred_element_type=F32
    )
    i, j = iota((tokens, tokens), 0), iota((tokens, tokens), 1)
    start_wide = jnp.concatenate([start] * (tokens // 128), axis=1)
    scores = jnp.where((j <= i) & (first + j >= start_wide), scores, 0.0)
    dt, cum = dt_ref[...], cum_ref[...]
    head_of = one_hot(128, inner, head_dim, 128)
    stepped = (spread(dt, head_of) * x_ref[...].astype(F32)).astype(BF16)
    cum_t = cum.T
    carry = jnp.where(start < first, jnp.exp(cum), 0.0)
    carry_ref[...] = spread(carry, head_of) * gate[...]
    each = 128 // head_dim
    for at in range(0, inner, 128):
        sums = []
        for h in range(at // head_dim, at // head_dim + each):
            gaps = jnp.minimum(cum[:, h : h + 1] - cum_t[h : h + 1, :], 0.0)
            weights = (jnp.exp(gaps) * scores).astype(BF16)
            sums.append(dot(weights, stepped[:, h * head_dim : (h + 1) * head_dim]))
        cut = slice(at, at + 128)
        direct = jnp.concatenate(sums, axis=1) + skip[:, cut] * x_ref[:, cut].astype(F32)
        direct_ref[:, cut] = direct * gate[:, cut]


def last_body(turn_ref, direct_ref, carry_ref, c_ref, carried_ref, out_w_ref, gain, *refs):
    *outs, held, lines, shares = refs
    tokens, inner = direct_ref.shape
    lines[...] = carried_ref[...].astype(F32)
    count = lines.shape[0] // LINES
    line = 0
    for row in range(0, held.shape[0], count):
        for at in range(0, inner, 128):
            cut = lines[pl.ds(line, count, stride=LINES), :]
            held[row : row + count, at : at + 128] = cut.astype(BF16)
            line += 1
    gated = direct_ref[...] + carry_ref[...] * dot(c_ref[...], held[...])
    scaled = (gated * gain[...]).astype(BF16)
    nt = (((1,), (1,)), ((), ()))
    features = shares.shape[2]
    for i in range(shares.shape[0]):
        rows = out_w_ref[i * features : (i + 1) * features]
        shares[i] = lax.dot_general(scaled, rows, nt, preferred_element_type=F32).astype(BF16)
    squares = lax.dot_general(
        jnp.ones((8, inner), F32),
        gated * gated,
        nt,
        precision=lax.Precision.HIGHEST,
        preferred_element_type=F32,
    )
    hi = squares.astype(BF16).astype(F32)
    row = iota(squares.shape, 0)
    riding = jnp.where(row == 0, hi, jnp.where(row == 1, squares - hi, 0.0)).astype(BF16)
    for d, out in enumerate(outs):
        out[:tokens] = shares[(turn_ref[0] + len(outs) - d) % len(outs)]
        out[tokens:, :tokens] = riding
        out[tokens:, tokens:] = jnp.zeros((8, features - tokens), BF16)


def on_device(
    hidden_in,
    w_in_gate,
    w_in_value,
    w_in_shared,
    w_in_step,
    conv_value,
    conv_shared,
    dt_bias,
    a_log,
    skip_gain,
    norm_gain,
    w_out,
    prompt_lengths,
    row_blocks,
):
    x_size, z_size, core_size = SIZES
    seq_count = x_size * z_size * core_size
    tp_count = lax.axis_size("tp")
    tokens, features = hidden_in.shape
    rows_here, inner = w_in_value.shape
    shared = w_in_shared.shape[1]
    heads = dt_bias.shape[0]
    head_dim = inner // heads
    state = shared // 2
    x_at, z_at, core_at = (lax.axis_index(name) for name in SEQ)
    tp_at = lax.axis_index("tp")
    seq_at = (x_at * z_size + z_at) * core_size + core_at

    x_shifts = list(range(1, x_size))

    def x_all(block):
        return [block] + [ahead(block, "x", d) for d in x_shifts]

    tie = lax.optimization_barrier

    before = lax.ppermute(
        hidden_in[tokens - EDGE :], SEQ, [(i, i + 1) for i in range(seq_count - 1)]
    )
    packed = pack(w_in_value, w_in_shared, w_in_step, w_in_gate, w_out.T)
    packed, before = tie((packed, before))
    along_z = lax.all_gather(packed, "z", axis=0, tiled=True)
    early_width = packed.shape[1] - 2 * inner - state
    own = x_all(along_z[:, :early_width])
    late = along_z[:, early_width:]
    mine = jnp.concatenate([before, hidden_in], axis=0)
    hidden = jnp.concatenate([mine] + [ahead(mine, "tp", d) for d in range(1, tp_count)], axis=1)

    chips = jnp.concatenate(
        [
            (x_at - d) % x_size * z_size + jnp.arange(z_size, dtype=jnp.int32)
            for d in range(x_size)
        ]
    )
    stored = jnp.concatenate([chips * core_size + core_at, chips * core_size + 1 - core_at])
    blocks_each = seq_count // tp_count
    model = jnp.take(row_blocks, stored)
    place = (tp_at - model // blocks_each) % tp_count * blocks_each + model % blocks_each
    h = jnp.take(hidden.reshape(hidden.shape[0], seq_count, rows_here), place, axis=1)
    h = h.reshape(hidden.shape[0], -1)
    own[-1], h, late = tie((own[-1], h, late))
    other = [ahead(block, "core", 1) for block in own]
    late_own = x_all(late)
    def lanes(row):
        return jnp.pad(row, (0, -row.shape[0] % 128))[None]

    first = jnp.reshape(seq_at * tokens, (1,))
    doc_ends = jnp.cumsum(prompt_lengths)
    rows, model_width = h.shape
    copies = state // seq_count
    x_rows, b_half, steps, cumulative, sent = call(
        functools.partial(early_body, head_dim),
        [
            ((tokens, inner), BF16),
            ((tokens, state), BF16),
            ((tokens, 128), F32),
            ((tokens, 128), F32),
            ((seq_count * LINES, 128), BF16),
        ],
        [first, doc_ends, h] + own + other + [conv_value, conv_shared, lanes(dt_bias), lanes(a_log)],
        scalars=2,
        scratch=[
            ((model_width, early_width), BF16),
            ((rows, early_width), F32),
            ((seq_count * LINES, 128), F32),
        ],
        flops=2 * rows * model_width * early_width,
    )
    received = lax.all_to_all(sent.reshape(seq_count, LINES, 128), SEQ, 0, 0, tiled=True)
    received, late_own = tie((received, late_own))
    (scanned,) = call(
        functools.partial(scan_body, head_dim, inner, copies),
        [((seq_count * LINES, 128), BF16)],
        [received.reshape(seq_count * LINES, 128)],
        scratch=[((seq_count * LINES, 128), F32)],
    )
    carried = lax.all_to_all(scanned.reshape(seq_count, LINES, 128), SEQ, 0, 0, tiled=True)
    carried = carried.reshape(seq_count * LINES, 128)
    late_other = [ahead(block, "core", 1) for block in late_own]
    direct, carry, c_half, out_w = call(
        functools.partial(middle_body, head_dim),
        [
            ((tokens, inner), F32),
            ((tokens, inner), F32),
            ((tokens, state), BF16),
            ((model_width, inner), BF16),
        ],
        [first, doc_ends, h]
        + late_own
        + late_other
        + [conv_shared, x_rows, b_half, steps, cumulative, jnp.repeat(skip_gain, head_dim)[None]],
        scalars=2,
        scratch=[
            ((model_width, inner + state), BF16),
            ((rows, state), F32),
            ((tokens, inner), F32),
        ],
        flops=2 * rows * model_width * (inner + state),
    )
    shares = call(
        last_body,
        [((tokens + 8, features), BF16)] * tp_count,
        [
            jnp.reshape(x_at - tp_at + tp_count, (1,)),
            direct,
            carry,
            c_half,
            carried,
            out_w,
            norm_gain[None],
        ],
        scalars=1,
        scratch=[
            ((state, inner), BF16),
            ((seq_count * LINES, 128), F32),
            ((tp_count, tokens, features), BF16),
        ],
        flops=2 * tokens * inner * model_width,
    )
    parts = [shares[0]] + [ahead(shares[d], "tp", d) for d in range(1, tp_count)]
    summed = sum(part.astype(F32) for part in parts)
    total = summed[tokens, :tokens] + summed[tokens + 1, :tokens]
    scale = lax.rsqrt(total / (inner * tp_count) + EPSILON)
    result = (summed[:tokens] * scale[:, None]).astype(BF16)

    lane = jnp.arange(features, dtype=jnp.int32)
    part, rest = lane // (z_size * rows_here), lane % (z_size * rows_here)
    core_of = jnp.where(part == 0, core_at, 1 - core_at)
    target = (rest // rows_here * core_size + core_of) * rows_here + rest % rows_here
    moves = (target[:, None] == lane[None, :]).astype(BF16)
    return jnp.dot(result, moves, preferred_element_type=F32).astype(BF16)


def solution(mesh):
    fine = Mesh(mesh.devices.reshape(SIZES + (-1,)), SEQ + ("tp",))
    return jax.shard_map(
        on_device,
        mesh=fine,
        in_specs=(
            P(SEQ, "tp"),
            P(SEQ, "tp"),
            P(SEQ, "tp"),
            P(SEQ, None),
            P(SEQ, "tp"),
            P(None, "tp"),
            P(),
            P("tp"),
            P("tp"),
            P("tp"),
            P("tp"),
            P("tp", SEQ),
            P(),
            P(),
        ),
        out_specs=P(SEQ, "tp"),
        check_vma=False,
    )
```

```python
import functools

import jax
import jax.numpy as jnp
from jax import lax
from jax.experimental import pallas as pl
from jax.experimental.pallas import tpu as pltpu
from jax.sharding import Mesh, PartitionSpec as P

EPSILON = 1e-05
EDGE = 8
LINES = 16
SEQ = ("x", "z", "core")
SIZES = (4, 8, 2)
BF16 = jnp.bfloat16
F32 = jnp.float32


def ahead(block, axis, distance):
    count = lax.axis_size(axis)
    return lax.ppermute(block, axis, [(i, (i + distance) % count) for i in range(count)])


def pack_body(value_ref, shared_ref, step_ref, gate_ref, out_t_ref, out_ref):
    inner, half, heads = value_ref.shape[1], shared_ref.shape[1] // 2, step_ref.shape[0]
    rest = -heads % 128
    step = jnp.pad(step_ref[...].T, ((0, 0), (0, rest)))
    at = 0
    for piece in (
        value_ref[...],
        shared_ref[:, :half],
        step,
        gate_ref[...],
        shared_ref[:, half:],
        out_t_ref[...],
    ):
        out_ref[:, at : at + piece.shape[1]] = piece.astype(BF16)
        at += piece.shape[1]


def pack(value, shared, step, gate, out_t):
    rows, inner = value.shape
    heads = step.shape[1]
    width = 3 * inner + shared.shape[1] + heads + -heads % 128
    return pl.pallas_call(
        pack_body,
        out_shape=jax.ShapeDtypeStruct((rows, width), BF16),
        in_specs=[pl.BlockSpec(memory_space=pltpu.VMEM)] * 5,
        out_specs=pl.BlockSpec(memory_space=pltpu.VMEM),
    )(value, shared, step.T, gate, out_t)


def call(
    body, shapes, args, scalars=0, blocks=0, near_in=0, near_out=0, scratch=(), flops=0, grant=60
):
    hbm, vmem = pl.BlockSpec(memory_space=pltpu.HBM), pl.BlockSpec(memory_space=pltpu.VMEM)
    fixed = scalars + blocks + near_in
    far_in, far_out = args[fixed:], shapes[near_out:]
    moved = sum(x.size * x.dtype.itemsize for x in args)

    def wrapped(*refs):
        ins, rest = refs[: len(args)], refs[len(args) :]
        outs, rest = rest[: len(shapes)], rest[len(shapes) :]
        held_in, rest = rest[: len(far_in)], rest[len(far_in) :]
        held_out, rest = rest[: len(far_out)], rest[len(far_out) :]
        *room, sems = rest
        copies = [
            pltpu.make_async_copy(src, dst, sems.at[i])
            for i, (src, dst) in enumerate(zip(ins[fixed:], held_in))
        ]
        for copy in copies:
            copy.start()
        free = sems.at[pl.ds(len(far_in) + len(far_out), blocks)] if blocks else None

        def ready():
            for copy in copies:
                copy.wait()

        body(ready, free, *ins[:fixed], *held_in, *outs[:near_out], *held_out, *room)
        copies_out = [
            pltpu.make_async_copy(src, dst, sems.at[len(far_in) + i])
            for i, (src, dst) in enumerate(zip(held_out, outs[near_out:]))
        ]
        for copy in copies_out:
            copy.start()
        for copy in copies_out:
            copy.wait()

    room = [pltpu.VMEM(x.shape, x.dtype) for x in far_in]
    room += [pltpu.VMEM(shape, kind) for shape, kind in far_out]
    room += [pltpu.VMEM(shape, kind) for shape, kind in scratch]
    room.append(pltpu.SemaphoreType.DMA((len(far_in) + len(far_out) + blocks,)))
    return pl.pallas_call(
        wrapped,
        out_shape=[jax.ShapeDtypeStruct(shape, kind) for shape, kind in shapes],
        in_specs=[pl.BlockSpec(memory_space=pltpu.SMEM)] * scalars
        + [hbm] * blocks
        + [vmem] * near_in
        + [hbm] * len(far_in),
        out_specs=[vmem] * near_out + [hbm] * len(far_out),
        scratch_shapes=room,
        compiler_params=pltpu.CompilerParams(vmem_limit_bytes=grant << 20),
        cost_estimate=pl.CostEstimate(flops=flops, bytes_accessed=moved, transcendentals=0),
    )(*args)


def dot(a, b, **kw):
    return jnp.dot(a, b, preferred_element_type=F32, **kw)


def iota(shape, dim):
    return lax.broadcasted_iota(jnp.int32, shape, dim)


def one_hot(rows, columns, width, wrap):
    return ((iota((rows, columns), 0) & (wrap - 1)) == iota((rows, columns), 1) // width).astype(BF16)


def spread(x, head_of):
    hi = x.astype(BF16)
    return dot(hi, head_of) + dot((x - hi.astype(F32)).astype(BF16), head_of)


def prompt_start(ends_ref, positions):
    start = jnp.zeros_like(positions)
    for i in range(ends_ref.shape[0]):
        start = jnp.maximum(start, jnp.where(positions >= ends_ref[i], ends_ref[i], 0))
    return start


def silu(x):
    return x / (1.0 + jnp.exp(-x))


def convolve(rows_ref, at, taps, positions, start):
    tokens, width = positions.shape[0], taps.shape[0]
    total = jnp.zeros(positions.shape, F32)
    for k in range(width):
        back = width - 1 - k
        rows = rows_ref[EDGE - back : EDGE - back + tokens, at : at + positions.shape[1]]
        total = total + jnp.where(positions - back >= start, taps[k : k + 1] * rows, 0.0)
    return silu(total).astype(BF16)


def fetch(blocks, held, sems, columns, order=None):
    depth = blocks[0].shape[0]
    copies = []
    for i, k in enumerate(order or range(len(blocks))):
        copy = pltpu.make_async_copy(
            blocks[k].at[:, columns], held.at[i * depth : (i + 1) * depth], sems.at[i]
        )
        copy.start()
        copies.append(copy)
    return copies


def arrange_body(block_rows, ready, sems, at_ref, order_ref, *refs):
    *pieces, edge_ref, h_ref, held = refs
    ready()
    x_at, core_at, tp_at = at_ref[0], at_ref[1], at_ref[2]
    tokens, features = pieces[0].shape
    x_size, z_size, core_size = SIZES
    for d, piece in enumerate(pieces):
        held[:tokens, d * features : (d + 1) * features] = piece[...]
    held[tokens:] = edge_ref[...]
    wide = h_ref.shape[1]
    each = features // block_rows
    lane = iota((8, wide), 1)
    block = lane // block_rows
    source = lane - block * block_rows
    count = 0
    for turn in range(core_size):
        for d in range(x_size):
            chip = ((x_at + x_size - d) & (x_size - 1)) * z_size
            for z in range(z_size):
                model = order_ref[(chip + z) * core_size + (core_at ^ turn)]
                piece = (tp_at + len(pieces) - model // each) & (len(pieces) - 1)
                base = (piece * each + (model & (each - 1))) * block_rows
                source = source + jnp.where(block == count, base, 0)
                count += 1
    for at in range(0, wide, 256):
        total = jnp.zeros((h_ref.shape[0], 256), F32)
        for k in range(0, wide, features):
            match = iota((features, 256), 0) + k == source[:1, at : at + 256]
            total = total + dot(held[:, k : k + features], match.astype(F32).astype(BF16))
        h_ref[:, at : at + 256] = total.astype(BF16)


def early_body(head_dim, ready, sems, first_ref, ends_ref, *refs):
    *blocks, h_ref, conv_value, conv_shared, bias, a_log = refs[:-8]
    x_ref, b_ref, dt_ref, cum_ref, sent_ref, held, rows, lines = refs[-8:]
    tokens, inner = x_ref.shape
    copies = fetch(blocks, held, sems, slice(0, held.shape[1]))
    ready()
    for copy in copies:
        copy.wait()
    for at in range(0, held.shape[1], 256):
        part = dot(h_ref[...], held[:, at : at + 256]).astype(BF16).astype(F32)
        rows[EDGE:, at : at + 256] = part[:tokens]
        rows[:EDGE, at : at + 256] = part[tokens:]
    first = first_ref[0]
    positions = first + iota((tokens, 128), 0)
    start = prompt_start(ends_ref, positions)
    last_start = prompt_start(ends_ref, first + tokens - 1)
    for at in range(0, inner, 128):
        x_ref[:, at : at + 128] = convolve(
            rows, at, conv_value[:, at : at + 128], positions, start
        )
    b_half = convolve(rows, inner, conv_shared[:, :128], positions, start)
    b_ref[...] = b_half
    raw = rows[EDGE:, inner + 128 :] + bias[...]
    dt = jnp.maximum(raw, 0.0) + jnp.log1p(jnp.exp(-jnp.abs(raw)))
    below = (iota((tokens, tokens), 0) >= iota((tokens, tokens), 1)).astype(F32)
    cum = dot(below, -dt * jnp.exp(a_log[...]), precision=lax.Precision.HIGHEST)
    dt_ref[...] = dt
    cum_ref[...] = cum
    last = cum[tokens - 1 :]
    tail = jnp.where(positions >= last_start, jnp.exp(last - cum), 0.0) * dt
    head_of = one_hot(128, inner, head_dim, 128)
    weighted = (spread(tail, head_of) * x_ref[...].astype(F32)).astype(BF16)
    fresh = dot(b_half.astype(F32).T.astype(BF16), weighted)
    lines[...] = jnp.zeros_like(lines)
    count = lines.shape[0] // LINES
    line = 0
    for row in range(0, fresh.shape[0], count):
        for at in range(0, inner, 128):
            lines[pl.ds(line, count, stride=LINES), :] = fresh[row : row + count, at : at + 128]
            line += 1
    keep = jnp.where(last_start < first, jnp.exp(last), 0.0)
    keep = jnp.broadcast_to(keep, (8, 128))
    keep_hi = keep.astype(BF16).astype(F32)
    keep_lo = pltpu.roll(keep - keep_hi, 64, axis=1)
    both = jnp.where(iota((8, 128), 1) < 64, keep_hi, keep_lo)
    lines[pl.ds(line, count, stride=LINES), :] = jnp.concatenate([both] * (count // 8), axis=0)
    sent_ref[...] = lines[...].astype(BF16)


def scan_body(head_dim, inner, copies, ready, sems, sent_ref, out_ref, lines):
    ready()
    lines[...] = sent_ref[...].astype(F32)
    count = lines.shape[0] // LINES
    tiles = inner // 128

    def line(r):
        return lines[pl.ds(r, count, stride=LINES), :]

    keeps = line(copies * tiles).astype(BF16)
    row = iota((count, 128), 0)

    def down(x, d):
        return jnp.where(row >= d, pltpu.roll(x, d, axis=0), 0.0)

    head_of = one_hot(128, inner, head_dim, 64)
    for t in range(tiles):
        keep = dot(keeps, head_of[:, t * 128 : (t + 1) * 128])
        states = [line(i * tiles + t) for i in range(copies)]
        d = 1
        while d < count:
            states = [x + keep * down(x, d) for x in states]
            keep = keep * down(keep, d)
            d *= 2
        for i, x in enumerate(states):
            lines[pl.ds(i * tiles + t, count, stride=LINES), :] = down(x, 1)
    out_ref[...] = lines[...].astype(BF16)


def middle_body(head_dim, ready, sems, first_ref, ends_ref, *refs):
    *blocks, h_ref, conv_shared, x_ref, b_ref, dt_ref, cum_ref, skip = refs[:-6]
    direct_ref, carry_ref, c_ref, held, c_rows, gate = refs[-6:]
    tokens, inner = x_ref.shape
    wide = held.shape[1]
    copies = fetch(blocks, held, sems, slice(0, wide))
    ready()
    for copy in copies:
        copy.wait()
    for at in range(0, inner, 256):
        g = dot(h_ref[:tokens], held[:, at : at + 256])
        gate[:, at : at + 256] = silu(g.astype(BF16).astype(F32))
    part = dot(h_ref[...], held[:, inner:]).astype(BF16).astype(F32)
    c_rows[EDGE:] = part[:tokens]
    c_rows[:EDGE] = part[tokens:]
    first = first_ref[0]
    positions = first + iota((tokens, 128), 0)
    start = prompt_start(ends_ref, positions)
    c_half = convolve(c_rows, 0, conv_shared[:, 128:], positions, start)
    c_ref[...] = c_half
    scores = lax.dot_general(
        c_half, b_ref[...], (((1,), (1,)), ((), ())), preferred_element_type=F32
    )
    i, j = iota((tokens, tokens), 0), iota((tokens, tokens), 1)
    start_wide = jnp.concatenate([start] * (tokens // 128), axis=1)
    scores = jnp.where((j <= i) & (first + j >= start_wide), scores, 0.0)
    dt, cum = dt_ref[...], cum_ref[...]
    head_of = one_hot(128, inner, head_dim, 128)
    stepped = (spread(dt, head_of) * x_ref[...].astype(F32)).astype(BF16)
    cum_t = cum.T
    carry = jnp.where(start < first, jnp.exp(cum), 0.0)
    carry_ref[...] = spread(carry, head_of) * gate[...]
    each = 128 // head_dim
    for at in range(0, inner, 128):
        sums = []
        for h in range(at // head_dim, at // head_dim + each):
            gaps = jnp.minimum(cum[:, h : h + 1] - cum_t[h : h + 1, :], 0.0)
            weights = (jnp.exp(gaps) * scores).astype(BF16)
            sums.append(dot(weights, stepped[:, h * head_dim : (h + 1) * head_dim]))
        cut = slice(at, at + 128)
        direct = jnp.concatenate(sums, axis=1) + skip[:, cut] * x_ref[:, cut].astype(F32)
        direct_ref[:, cut] = direct * gate[:, cut]


def last_body(ready, sems, turn_ref, *refs):
    *blocks, carried_ref, direct_ref, carry_ref, c_ref, gain = refs[:-8]
    *outs, held, lines, shares, out_w = refs[-8:]
    half, wide = len(blocks) // 2, blocks[0].shape[1]
    order = [i + half * j for i in range(half) for j in (0, 1)]
    copies = fetch(blocks, out_w, sems, slice(wide - out_w.shape[1], wide), order=order)
    ready()
    tokens, inner = direct_ref.shape
    lines[...] = carried_ref[...].astype(F32)
    count = lines.shape[0] // LINES
    line = 0
    for row in range(0, held.shape[0], count):
        for at in range(0, inner, 128):
            cut = lines[pl.ds(line, count, stride=LINES), :]
            held[row : row + count, at : at + 128] = cut.astype(BF16)
            line += 1
    gated = direct_ref[...] + carry_ref[...] * dot(c_ref[...], held[...])
    scaled = (gated * gain[...]).astype(BF16)
    nt = (((1,), (1,)), ((), ()))
    features = shares.shape[2]
    for copy in copies:
        copy.wait()
    for i in range(shares.shape[0]):
        rows = out_w[i * features : (i + 1) * features]
        shares[i] = lax.dot_general(scaled, rows, nt, preferred_element_type=F32).astype(BF16)
    squares = lax.dot_general(
        jnp.ones((8, inner), F32),
        gated * gated,
        nt,
        precision=lax.Precision.HIGHEST,
        preferred_element_type=F32,
    )
    hi = squares.astype(BF16).astype(F32)
    row = iota(squares.shape, 0)
    riding = jnp.where(row == 0, hi, jnp.where(row == 1, squares - hi, 0.0)).astype(BF16)
    for d, out in enumerate(outs):
        out[:tokens] = shares[(turn_ref[0] + len(outs) - d) % len(outs)]
        out[tokens:, :tokens] = riding
        out[tokens:, tokens:] = jnp.zeros((8, features - tokens), BF16)


def on_device(
    hidden_in,
    w_in_gate,
    w_in_value,
    w_in_shared,
    w_in_step,
    conv_value,
    conv_shared,
    dt_bias,
    a_log,
    skip_gain,
    norm_gain,
    w_out,
    prompt_lengths,
    row_blocks,
):
    x_size, z_size, core_size = SIZES
    seq_count = x_size * z_size * core_size
    tp_count = lax.axis_size("tp")
    tokens, features = hidden_in.shape
    rows_here, inner = w_in_value.shape
    shared = w_in_shared.shape[1]
    heads = dt_bias.shape[0]
    head_dim = inner // heads
    state = shared // 2
    x_at, z_at, core_at = (lax.axis_index(name) for name in SEQ)
    tp_at = lax.axis_index("tp")
    seq_at = (x_at * z_size + z_at) * core_size + core_at

    x_shifts = list(range(1, x_size))

    def x_all(block):
        return [block] + [ahead(block, "x", d) for d in x_shifts]

    tie = lax.optimization_barrier

    pieces = [hidden_in] + [ahead(hidden_in, "tp", d) for d in range(1, tp_count)]
    packed = pack(w_in_value, w_in_shared, w_in_step, w_in_gate, w_out.T)
    along_z = lax.all_gather(packed, "z", axis=0, tiled=True)
    early_width = packed.shape[1] - 2 * inner - state
    own = x_all(along_z[:, :early_width])
    late = along_z[:, early_width:]
    edge = jnp.concatenate([piece[tokens - EDGE :] for piece in pieces], axis=1)
    edge = lax.ppermute(edge, SEQ, [(i, i + 1) for i in range(seq_count - 1)])
    rows, model_width = tokens + EDGE, features * tp_count
    (h,) = call(
        functools.partial(arrange_body, rows_here),
        [((rows, model_width), BF16)],
        [jnp.stack([x_at, core_at, tp_at]), row_blocks] + pieces + [edge],
        scalars=2,
        scratch=[((rows, model_width), BF16)],
        flops=2 * rows * model_width * model_width,
    )
    own[-1], h, late = tie((own[-1], h, late))
    other = [ahead(block, "core", 1) for block in own]
    late_own = x_all(late)

    def lanes(row):
        return jnp.pad(row, (0, -row.shape[0] % 128))[None]

    first = jnp.reshape(seq_at * tokens, (1,))
    doc_ends = jnp.cumsum(prompt_lengths)
    copies = state // seq_count
    x_rows, b_half, steps, cumulative, sent = call(
        functools.partial(early_body, head_dim),
        [
            ((tokens, inner), BF16),
            ((tokens, state), BF16),
            ((tokens, 128), F32),
            ((tokens, 128), F32),
            ((seq_count * LINES, 128), BF16),
        ],
        [first, doc_ends] + own + other + [h, conv_value, conv_shared, lanes(dt_bias), lanes(a_log)],
        scalars=2,
        blocks=len(own + other),
        scratch=[
            ((model_width, early_width), BF16),
            ((rows, early_width), F32),
            ((seq_count * LINES, 128), F32),
        ],
        flops=2 * rows * model_width * early_width,
    )
    received = lax.all_to_all(sent.reshape(seq_count, LINES, 128), SEQ, 0, 0, tiled=True)
    (scanned,) = call(
        functools.partial(scan_body, head_dim, inner, copies),
        [((seq_count * LINES, 128), BF16)],
        [received.reshape(seq_count * LINES, 128)],
        near_in=1,
        grant=40,
        scratch=[((seq_count * LINES, 128), F32)],
    )
    carried = lax.all_to_all(scanned.reshape(seq_count, LINES, 128), SEQ, 0, 0, tiled=True)
    carried = carried.reshape(seq_count * LINES, 128)
    late_other = [ahead(block, "core", 1) for block in late_own]
    direct, carry, c_half = call(
        functools.partial(middle_body, head_dim),
        [
            ((tokens, inner), F32),
            ((tokens, inner), F32),
            ((tokens, state), BF16),
        ],
        [first, doc_ends]
        + late_own
        + late_other
        + [h, conv_shared, x_rows, b_half, steps, cumulative, jnp.repeat(skip_gain, head_dim)[None]],
        scalars=2,
        blocks=len(late_own + late_other),
        near_out=3,
        scratch=[
            ((model_width, inner + state), BF16),
            ((rows, state), F32),
            ((tokens, inner), F32),
        ],
        flops=2 * rows * model_width * (inner + state),
    )
    shares = call(
        last_body,
        [((tokens + 8, features), BF16)] * tp_count,
        [
            jnp.reshape(x_at - tp_at + tp_count, (1,)),
            *late_own,
            *late_other,
            carried,
            direct,
            carry,
            c_half,
            norm_gain[None],
        ],
        scalars=1,
        blocks=len(late_own + late_other),
        near_in=4,
        scratch=[
            ((state, inner), BF16),
            ((seq_count * LINES, 128), F32),
            ((tp_count, tokens, features), BF16),
            ((model_width, inner), BF16),
        ],
        flops=2 * tokens * inner * model_width,
    )
    parts = [shares[0]] + [ahead(shares[d], "tp", d) for d in range(1, tp_count)]
    summed = sum(part.astype(F32) for part in parts)
    total = summed[tokens, :tokens] + summed[tokens + 1, :tokens]
    scale = lax.rsqrt(total / (inner * tp_count) + EPSILON)
    result = (summed[:tokens] * scale[:, None]).astype(BF16)

    lane = jnp.arange(features, dtype=jnp.int32)
    part, rest = lane // (z_size * rows_here), lane % (z_size * rows_here)
    core_of = jnp.where(part == 0, core_at, 1 - core_at)
    target = (rest // rows_here * core_size + core_of) * rows_here + rest % rows_here
    moves = (target[:, None] == lane[None, :]).astype(BF16)
    return jnp.dot(result, moves, preferred_element_type=F32).astype(BF16)


def solution(mesh):
    fine = Mesh(mesh.devices.reshape(SIZES + (-1,)), SEQ + ("tp",))
    return jax.shard_map(
        on_device,
        mesh=fine,
        in_specs=(
            P(SEQ, "tp"),
            P(SEQ, "tp"),
            P(SEQ, "tp"),
            P(SEQ, None),
            P(SEQ, "tp"),
            P(None, "tp"),
            P(),
            P("tp"),
            P("tp"),
            P("tp"),
            P("tp"),
            P("tp", SEQ),
            P(),
            P(),
        ),
        out_specs=P(SEQ, "tp"),
        check_vma=False,
    )
```

```python
import functools

import jax
import jax.numpy as jnp
from jax import lax
from jax.experimental import pallas as pl
from jax.experimental.pallas import tpu as pltpu
from jax.sharding import Mesh, PartitionSpec as P

EPSILON = 1e-05
EDGE = 8
LINES = 16
SEQ = ("x", "z", "core")
SIZES = (4, 8, 2)
BF16 = jnp.bfloat16
F32 = jnp.float32


def ahead(block, axis, distance):
    count = lax.axis_size(axis)
    return lax.ppermute(block, axis, [(i, (i + distance) % count) for i in range(count)])


def pack_body(value_ref, shared_ref, step_ref, gate_ref, out_t_ref, out_ref):
    inner, half, heads = value_ref.shape[1], shared_ref.shape[1] // 2, step_ref.shape[0]
    rest = -heads % 128
    step = jnp.pad(step_ref[...].T, ((0, 0), (0, rest)))
    at = 0
    for piece in (
        value_ref[...],
        shared_ref[:, :half],
        step,
        gate_ref[...],
        shared_ref[:, half:],
        out_t_ref[...],
    ):
        out_ref[:, at : at + piece.shape[1]] = piece.astype(BF16)
        at += piece.shape[1]


def pack(value, shared, step, gate, out_t):
    rows, inner = value.shape
    heads = step.shape[1]
    width = 3 * inner + shared.shape[1] + heads + -heads % 128
    return pl.pallas_call(
        pack_body,
        out_shape=jax.ShapeDtypeStruct((rows, width), BF16),
        in_specs=[pl.BlockSpec(memory_space=pltpu.VMEM)] * 5,
        out_specs=pl.BlockSpec(memory_space=pltpu.VMEM),
    )(value, shared, step.T, gate, out_t)


def call(
    body, shapes, args, scalars=0, blocks=0, near_in=0, near_out=0, scratch=(), flops=0, grant=60
):
    hbm, vmem = pl.BlockSpec(memory_space=pltpu.HBM), pl.BlockSpec(memory_space=pltpu.VMEM)
    fixed = scalars + blocks + near_in
    far_in, far_out = args[fixed:], shapes[near_out:]
    moved = sum(x.size * x.dtype.itemsize for x in args)

    def wrapped(*refs):
        ins, rest = refs[: len(args)], refs[len(args) :]
        outs, rest = rest[: len(shapes)], rest[len(shapes) :]
        held_in, rest = rest[: len(far_in)], rest[len(far_in) :]
        held_out, rest = rest[: len(far_out)], rest[len(far_out) :]
        *room, sems = rest
        copies = [
            pltpu.make_async_copy(src, dst, sems.at[i])
            for i, (src, dst) in enumerate(zip(ins[fixed:], held_in))
        ]
        for copy in copies:
            copy.start()
        free = sems.at[pl.ds(len(far_in) + len(far_out), blocks)] if blocks else None

        def ready():
            for copy in copies:
                copy.wait()

        body(ready, free, *ins[:fixed], *held_in, *outs[:near_out], *held_out, *room)
        copies_out = [
            pltpu.make_async_copy(src, dst, sems.at[len(far_in) + i])
            for i, (src, dst) in enumerate(zip(held_out, outs[near_out:]))
        ]
        for copy in copies_out:
            copy.start()
        for copy in copies_out:
            copy.wait()

    room = [pltpu.VMEM(x.shape, x.dtype) for x in far_in]
    room += [pltpu.VMEM(shape, kind) for shape, kind in far_out]
    room += [pltpu.VMEM(shape, kind) for shape, kind in scratch]
    room.append(pltpu.SemaphoreType.DMA((len(far_in) + len(far_out) + blocks,)))
    return pl.pallas_call(
        wrapped,
        out_shape=[jax.ShapeDtypeStruct(shape, kind) for shape, kind in shapes],
        in_specs=[pl.BlockSpec(memory_space=pltpu.SMEM)] * scalars
        + [hbm] * blocks
        + [vmem] * near_in
        + [hbm] * len(far_in),
        out_specs=[vmem] * near_out + [hbm] * len(far_out),
        scratch_shapes=room,
        compiler_params=pltpu.CompilerParams(vmem_limit_bytes=grant << 20),
        cost_estimate=pl.CostEstimate(flops=flops, bytes_accessed=moved, transcendentals=0),
    )(*args)


def dot(a, b, **kw):
    return jnp.dot(a, b, preferred_element_type=F32, **kw)


def iota(shape, dim):
    return lax.broadcasted_iota(jnp.int32, shape, dim)


def one_hot(rows, columns, width, wrap):
    return ((iota((rows, columns), 0) & (wrap - 1)) == iota((rows, columns), 1) // width).astype(BF16)


def spread(x, head_of):
    hi = x.astype(BF16)
    return dot(hi, head_of) + dot((x - hi.astype(F32)).astype(BF16), head_of)


def prompt_start(lengths_ref, positions):
    start, end = jnp.zeros_like(positions), 0
    for i in range(lengths_ref.shape[0]):
        end = end + lengths_ref[i]
        start = jnp.maximum(start, jnp.where(positions >= end, end, 0))
    return start


def lanes(row):
    return jnp.pad(row, ((0, 0), (0, -row.shape[1] % 128)))


def silu(x):
    return x / (1.0 + jnp.exp(-x))


def convolve(rows_ref, at, taps, positions, start):
    tokens, width = positions.shape[0], taps.shape[0]
    total = jnp.zeros(positions.shape, F32)
    for k in range(width):
        back = width - 1 - k
        rows = rows_ref[EDGE - back : EDGE - back + tokens, at : at + positions.shape[1]]
        total = total + jnp.where(positions - back >= start, taps[k : k + 1] * rows, 0.0)
    return silu(total).astype(BF16)


def fetch(blocks, held, sems, columns, order=None):
    depth = blocks[0].shape[0]
    copies = []
    for i, k in enumerate(order or range(len(blocks))):
        copy = pltpu.make_async_copy(
            blocks[k].at[:, columns], held.at[i * depth : (i + 1) * depth], sems.at[i]
        )
        copy.start()
        copies.append(copy)
    return copies


def arrange_body(block_rows, ready, sems, at_ref, order_ref, *refs):
    *pieces, edge_ref, h_ref, held = refs
    ready()
    x_at, core_at, tp_at = at_ref[0], at_ref[1], at_ref[2]
    tokens, features = pieces[0].shape
    x_size, z_size, core_size = SIZES
    for d, piece in enumerate(pieces):
        held[:tokens, d * features : (d + 1) * features] = piece[...]
    held[tokens:] = edge_ref[...]
    wide = h_ref.shape[1]
    each = features // block_rows
    lane = iota((8, wide), 1)
    block = lane // block_rows
    source = lane - block * block_rows
    count = 0
    for turn in range(core_size):
        for d in range(x_size):
            chip = ((x_at + x_size - d) & (x_size - 1)) * z_size
            for z in range(z_size):
                model = order_ref[(chip + z) * core_size + (core_at ^ turn)]
                piece = (tp_at + len(pieces) - model // each) & (len(pieces) - 1)
                base = (piece * each + (model & (each - 1))) * block_rows
                source = source + jnp.where(block == count, base, 0)
                count += 1
    for at in range(0, wide, 256):
        total = jnp.zeros((h_ref.shape[0], 256), F32)
        for k in range(0, wide, features):
            match = iota((features, 256), 0) + k == source[:1, at : at + 256]
            total = total + dot(held[:, k : k + features], match.astype(F32).astype(BF16))
        h_ref[:, at : at + 256] = total.astype(BF16)


def early_body(head_dim, ready, sems, first_ref, lengths_ref, *refs):
    *blocks, h_ref, conv_value, conv_shared, bias, a_log = refs[:-8]
    x_ref, b_ref, dt_ref, cum_ref, sent_ref, held, rows, lines = refs[-8:]
    tokens, inner = x_ref.shape
    copies = fetch(blocks, held, sems, slice(0, held.shape[1]))
    ready()
    for copy in copies:
        copy.wait()
    for at in range(0, held.shape[1], 256):
        part = dot(h_ref[...], held[:, at : at + 256]).astype(BF16).astype(F32)
        rows[EDGE:, at : at + 256] = part[:tokens]
        rows[:EDGE, at : at + 256] = part[tokens:]
    first = first_ref[0]
    positions = first + iota((tokens, 128), 0)
    start = prompt_start(lengths_ref, positions)
    last_start = prompt_start(lengths_ref, first + tokens - 1)
    for at in range(0, inner, 128):
        x_ref[:, at : at + 128] = convolve(
            rows, at, conv_value[:, at : at + 128], positions, start
        )
    b_half = convolve(rows, inner, conv_shared[:, :128], positions, start)
    b_ref[...] = b_half
    raw = rows[EDGE:, inner + 128 :] + lanes(bias[...])
    dt = jnp.maximum(raw, 0.0) + jnp.log1p(jnp.exp(-jnp.abs(raw)))
    below = (iota((tokens, tokens), 0) >= iota((tokens, tokens), 1)).astype(F32)
    cum = dot(below, -dt * jnp.exp(lanes(a_log[...])), precision=lax.Precision.HIGHEST)
    dt_ref[...] = dt
    cum_ref[...] = cum
    last = cum[tokens - 1 :]
    tail = jnp.where(positions >= last_start, jnp.exp(last - cum), 0.0) * dt
    head_of = one_hot(128, inner, head_dim, 128)
    weighted = (spread(tail, head_of) * x_ref[...].astype(F32)).astype(BF16)
    fresh = dot(b_half.astype(F32).T.astype(BF16), weighted)
    lines[...] = jnp.zeros_like(lines)
    count = lines.shape[0] // LINES
    line = 0
    for row in range(0, fresh.shape[0], count):
        for at in range(0, inner, 128):
            lines[pl.ds(line, count, stride=LINES), :] = fresh[row : row + count, at : at + 128]
            line += 1
    keep = jnp.where(last_start < first, jnp.exp(last), 0.0)
    keep = jnp.broadcast_to(keep, (8, 128))
    keep_hi = keep.astype(BF16).astype(F32)
    keep_lo = pltpu.roll(keep - keep_hi, 64, axis=1)
    both = jnp.where(iota((8, 128), 1) < 64, keep_hi, keep_lo)
    lines[pl.ds(line, count, stride=LINES), :] = jnp.concatenate([both] * (count // 8), axis=0)
    sent_ref[...] = lines[...].astype(BF16)


def scan_body(head_dim, inner, copies, ready, sems, sent_ref, out_ref, lines):
    ready()
    lines[...] = sent_ref[...].astype(F32)
    count = lines.shape[0] // LINES
    tiles = inner // 128

    def line(r):
        return lines[pl.ds(r, count, stride=LINES), :]

    keeps = line(copies * tiles).astype(BF16)
    row = iota((count, 128), 0)

    def down(x, d):
        return jnp.where(row >= d, pltpu.roll(x, d, axis=0), 0.0)

    head_of = one_hot(128, inner, head_dim, 64)
    for t in range(tiles):
        keep = dot(keeps, head_of[:, t * 128 : (t + 1) * 128])
        states = [line(i * tiles + t) for i in range(copies)]
        d = 1
        while d < count:
            states = [x + keep * down(x, d) for x in states]
            keep = keep * down(keep, d)
            d *= 2
        for i, x in enumerate(states):
            lines[pl.ds(i * tiles + t, count, stride=LINES), :] = down(x, 1)
    out_ref[...] = lines[...].astype(BF16)


def middle_body(head_dim, ready, sems, first_ref, lengths_ref, *refs):
    *blocks, h_ref, conv_shared, x_ref, b_ref, dt_ref, cum_ref, skip = refs[:-6]
    direct_ref, carry_ref, c_ref, held, c_rows, gate = refs[-6:]
    tokens, inner = x_ref.shape
    wide = held.shape[1]
    copies = fetch(blocks, held, sems, slice(0, wide))
    ready()
    for copy in copies:
        copy.wait()
    for at in range(0, inner, 256):
        g = dot(h_ref[:tokens], held[:, at : at + 256])
        gate[:, at : at + 256] = silu(g.astype(BF16).astype(F32))
    part = dot(h_ref[...], held[:, inner:]).astype(BF16).astype(F32)
    c_rows[EDGE:] = part[:tokens]
    c_rows[:EDGE] = part[tokens:]
    first = first_ref[0]
    positions = first + iota((tokens, 128), 0)
    start = prompt_start(lengths_ref, positions)
    c_half = convolve(c_rows, 0, conv_shared[:, 128:], positions, start)
    c_ref[...] = c_half
    scores = lax.dot_general(
        c_half, b_ref[...], (((1,), (1,)), ((), ())), preferred_element_type=F32
    )
    i, j = iota((tokens, tokens), 0), iota((tokens, tokens), 1)
    start_wide = jnp.concatenate([start] * (tokens // 128), axis=1)
    scores = jnp.where((j <= i) & (first + j >= start_wide), scores, 0.0)
    dt, cum = dt_ref[...], cum_ref[...]
    head_of = one_hot(128, inner, head_dim, 128)
    stepped = (spread(dt, head_of) * x_ref[...].astype(F32)).astype(BF16)
    cum_t = cum.T
    carry = jnp.where(start < first, jnp.exp(cum), 0.0)
    carry_ref[...] = (spread(carry, head_of) * gate[...]).astype(BF16)
    each = 128 // head_dim
    for at in range(0, inner, 128):
        sums = []
        for h in range(at // head_dim, at // head_dim + each):
            gaps = jnp.minimum(cum[:, h : h + 1] - cum_t[h : h + 1, :], 0.0)
            weights = (jnp.exp(gaps) * scores).astype(BF16)
            sums.append(dot(weights, stepped[:, h * head_dim : (h + 1) * head_dim]))
        cut = slice(at, at + 128)
        direct = jnp.concatenate(sums, axis=1) + skip[:, cut] * x_ref[:, cut].astype(F32)
        direct_ref[:, cut] = (direct * gate[:, cut]).astype(BF16)


def last_body(ready, sems, turn_ref, *refs):
    *blocks, carried_ref, direct_ref, carry_ref, c_ref, gain = refs[:-8]
    *outs, held, lines, shares, out_w = refs[-8:]
    half, wide, inner = len(blocks) // 2, blocks[0].shape[2], out_w.shape[4]
    copies = []
    for i, block in enumerate(blocks):
        copy = pltpu.make_async_copy(
            block.at[:, :, wide - inner :],
            out_w.at[i % half, :, turn_ref[1] ^ (i // half)],
            sems.at[i],
        )
        copy.start()
        copies.append(copy)
    ready()
    tokens, inner = direct_ref.shape
    lines[...] = carried_ref[...].astype(F32)
    count = lines.shape[0] // LINES
    line = 0
    for row in range(0, held.shape[0], count):
        for at in range(0, inner, 128):
            cut = lines[pl.ds(line, count, stride=LINES), :]
            held[row : row + count, at : at + 128] = cut.astype(BF16)
            line += 1
    direct, carry = direct_ref[...].astype(F32), carry_ref[...].astype(F32)
    gated = direct + carry * dot(c_ref[...], held[...])
    scaled = (gated * gain[...]).astype(BF16)
    nt = (((1,), (1,)), ((), ()))
    features = shares.shape[2]
    for copy in copies:
        copy.wait()
    for i in range(shares.shape[0]):
        rows = out_w[i].reshape(features, inner)
        shares[i] = lax.dot_general(scaled, rows, nt, preferred_element_type=F32).astype(BF16)
    squares = lax.dot_general(
        jnp.ones((8, inner), F32),
        gated * gated,
        nt,
        precision=lax.Precision.HIGHEST,
        preferred_element_type=F32,
    )
    hi = squares.astype(BF16).astype(F32)
    row = iota(squares.shape, 0)
    riding = jnp.where(row == 0, hi, jnp.where(row == 1, squares - hi, 0.0)).astype(BF16)
    for d, out in enumerate(outs):
        out[:tokens] = shares[(turn_ref[0] + len(outs) - d) % len(outs)]
        out[tokens:, :tokens] = riding
        out[tokens:, tokens:] = jnp.zeros((8, features - tokens), BF16)


def on_device(
    hidden_in,
    w_in_gate,
    w_in_value,
    w_in_shared,
    w_in_step,
    conv_value,
    conv_shared,
    dt_bias,
    a_log,
    skip_gain,
    norm_gain,
    w_out,
    prompt_lengths,
    row_blocks,
):
    x_size, z_size, core_size = SIZES
    seq_count = x_size * z_size * core_size
    tp_count = lax.axis_size("tp")
    tokens, features = hidden_in.shape
    rows_here, inner = w_in_value.shape
    shared = w_in_shared.shape[1]
    heads = dt_bias.shape[0]
    head_dim = inner // heads
    state = shared // 2
    x_at, z_at, core_at = (lax.axis_index(name) for name in SEQ)
    tp_at = lax.axis_index("tp")
    seq_at = (x_at * z_size + z_at) * core_size + core_at

    x_shifts = list(range(1, x_size))

    def x_all(block):
        return [block] + [ahead(block, "x", d) for d in x_shifts]

    tie = lax.optimization_barrier

    pieces = [hidden_in] + [ahead(hidden_in, "tp", d) for d in range(1, tp_count)]
    packed = pack(w_in_value, w_in_shared, w_in_step, w_in_gate, w_out.T)
    along_z = lax.all_gather(packed, "z", axis=0, tiled=True)
    early_width = packed.shape[1] - 2 * inner - state
    own = x_all(along_z[:, :early_width])
    late = along_z[:, early_width:]
    edge = jnp.concatenate([piece[tokens - EDGE :] for piece in pieces], axis=1)
    edge = lax.ppermute(edge, SEQ, [(i, i + 1) for i in range(seq_count - 1)])
    rows, model_width = tokens + EDGE, features * tp_count
    (h,) = call(
        functools.partial(arrange_body, rows_here),
        [((rows, model_width), BF16)],
        [jnp.stack([x_at, core_at, tp_at]), row_blocks] + pieces + [edge],
        scalars=2,
        scratch=[((rows, model_width), BF16)],
        flops=2 * rows * model_width * model_width,
    )
    own[-1], h, late = tie((own[-1], h, late))
    other = [ahead(block, "core", 1) for block in own]
    late_own = x_all(late)

    first = jnp.reshape(seq_at * tokens, (1,))
    copies = state // seq_count
    x_rows, b_half, steps, cumulative, sent = call(
        functools.partial(early_body, head_dim),
        [
            ((tokens, inner), BF16),
            ((tokens, state), BF16),
            ((tokens, 128), F32),
            ((tokens, 128), F32),
            ((seq_count * LINES, 128), BF16),
        ],
        [first, prompt_lengths] + own + other + [h, conv_value, conv_shared, dt_bias[None], a_log[None]],
        scalars=2,
        blocks=len(own + other),
        scratch=[
            ((model_width, early_width), BF16),
            ((rows, early_width), F32),
            ((seq_count * LINES, 128), F32),
        ],
        flops=2 * rows * model_width * early_width,
    )
    received = lax.all_to_all(sent.reshape(seq_count, LINES, 128), SEQ, 0, 0, tiled=True)
    (scanned,) = call(
        functools.partial(scan_body, head_dim, inner, copies),
        [((seq_count * LINES, 128), BF16)],
        [received.reshape(seq_count * LINES, 128)],
        near_in=1,
        grant=40,
        scratch=[((seq_count * LINES, 128), F32)],
    )
    carried = lax.all_to_all(scanned.reshape(seq_count, LINES, 128), SEQ, 0, 0, tiled=True)
    carried = carried.reshape(seq_count * LINES, 128)
    late_own, _ = tie((late_own, scanned))
    late_other = [ahead(block, "core", 1) for block in late_own]
    direct, carry, c_half = call(
        functools.partial(middle_body, head_dim),
        [
            ((tokens, inner), BF16),
            ((tokens, inner), BF16),
            ((tokens, state), BF16),
        ],
        [first, prompt_lengths]
        + late_own
        + late_other
        + [h, conv_shared, x_rows, b_half, steps, cumulative, jnp.repeat(skip_gain, head_dim)[None]],
        scalars=2,
        blocks=len(late_own + late_other),
        scratch=[
            ((model_width, inner + state), BF16),
            ((rows, state), F32),
            ((tokens, inner), F32),
        ],
        flops=2 * rows * model_width * (inner + state),
    )
    shares = call(
        last_body,
        [((tokens + 8, features), BF16)] * tp_count,
        [
            jnp.stack([x_at - tp_at + tp_count, core_at]),
            *[block.reshape(z_size, rows_here, -1) for block in late_own + late_other],
            carried,
            direct,
            carry,
            c_half,
            norm_gain[None],
        ],
        scalars=1,
        blocks=len(late_own + late_other),
        scratch=[
            ((state, inner), BF16),
            ((seq_count * LINES, 128), F32),
            ((tp_count, tokens, features), BF16),
            ((x_size, z_size, core_size, rows_here, inner), BF16),
        ],
        flops=2 * tokens * inner * model_width,
    )
    parts = [shares[0]] + [ahead(shares[d], "tp", d) for d in range(1, tp_count)]
    summed = sum(part.astype(F32) for part in parts)
    total = summed[tokens, :tokens] + summed[tokens + 1, :tokens]
    scale = lax.rsqrt(total / (inner * tp_count) + EPSILON)
    return (summed[:tokens] * scale[:, None]).astype(BF16)


def solution(mesh):
    fine = Mesh(mesh.devices.reshape(SIZES + (-1,)), SEQ + ("tp",))
    return jax.shard_map(
        on_device,
        mesh=fine,
        in_specs=(
            P(SEQ, "tp"),
            P(SEQ, "tp"),
            P(SEQ, "tp"),
            P(SEQ, None),
            P(SEQ, "tp"),
            P(None, "tp"),
            P(),
            P("tp"),
            P("tp"),
            P("tp"),
            P("tp"),
            P("tp", SEQ),
            P(),
            P(),
        ),
        out_specs=P(SEQ, "tp"),
        check_vma=False,
    )
```

```python
import functools

import jax
import jax.numpy as jnp
from jax import lax
from jax.experimental import pallas as pl
from jax.experimental.pallas import tpu as pltpu
from jax.sharding import Mesh, PartitionSpec as P

EPSILON = 1e-05
EDGE = 8
LINES = 16
SEQ = ("x", "z", "core")
SIZES = (4, 8, 2)
BF16 = jnp.bfloat16
F32 = jnp.float32


def ahead(block, axis, distance):
    count = lax.axis_size(axis)
    return lax.ppermute(block, axis, [(i, (i + distance) % count) for i in range(count)])


def pack_body(value_ref, shared_ref, step_ref, out_ref):
    inner, half, heads = value_ref.shape[1], shared_ref.shape[1] // 2, step_ref.shape[0]
    out_ref[:, :inner] = value_ref[...].astype(BF16)
    out_ref[:, inner : inner + half] = shared_ref[:, :half].astype(BF16)
    step = jnp.pad(step_ref[...].T, ((0, 0), (0, -heads % 128)))
    out_ref[:, inner + half :] = step.astype(BF16)


def pack_late_body(gate_ref, shared_ref, out_t_ref, out_ref):
    inner, half = gate_ref.shape[1], shared_ref.shape[1] // 2
    out_ref[:, :inner] = gate_ref[...].astype(BF16)
    out_ref[:, inner : inner + half] = shared_ref[:, half:].astype(BF16)
    out_ref[:, inner + half :] = out_t_ref[...].astype(BF16)


def pack(body, width, *args):
    return pl.pallas_call(
        body,
        out_shape=jax.ShapeDtypeStruct((args[0].shape[0], width), BF16),
        in_specs=[pl.BlockSpec(memory_space=pltpu.VMEM)] * 3,
        out_specs=pl.BlockSpec(memory_space=pltpu.VMEM),
    )(*args)


def call(
    body, shapes, args, scalars=0, blocks=0, near_in=0, near_out=0, sent=0, scratch=(), flops=0, grant=60
):
    hbm, vmem = pl.BlockSpec(memory_space=pltpu.HBM), pl.BlockSpec(memory_space=pltpu.VMEM)
    any_space = pl.BlockSpec(memory_space=pl.ANY)
    fixed = scalars + blocks + near_in
    near_out = near_out + sent
    far_in, far_out = args[fixed:], shapes[near_out:]
    moved = sum(x.size * x.dtype.itemsize for x in args)

    def wrapped(*refs):
        ins, rest = refs[: len(args)], refs[len(args) :]
        outs, rest = rest[: len(shapes)], rest[len(shapes) :]
        held_in, rest = rest[: len(far_in)], rest[len(far_in) :]
        held_out, rest = rest[: len(far_out)], rest[len(far_out) :]
        *room, sems = rest
        copies = [
            pltpu.make_async_copy(src, dst, sems.at[i])
            for i, (src, dst) in enumerate(zip(ins[fixed:], held_in))
        ]
        for copy in copies:
            copy.start()
        free = sems.at[pl.ds(len(far_in) + len(far_out), blocks)] if blocks else None

        def ready():
            for copy in copies:
                copy.wait()

        body(ready, free, *ins[:fixed], *held_in, *outs[:near_out], *held_out, *room)
        copies_out = [
            pltpu.make_async_copy(src, dst, sems.at[len(far_in) + i])
            for i, (src, dst) in enumerate(zip(held_out, outs[near_out:]))
        ]
        for copy in copies_out:
            copy.start()
        for copy in copies_out:
            copy.wait()

    room = [pltpu.VMEM(x.shape, x.dtype) for x in far_in]
    room += [pltpu.VMEM(shape, kind) for shape, kind in far_out]
    room += [pltpu.VMEM(shape, kind) for shape, kind in scratch]
    if sent:
        room.append(pltpu.SemaphoreType.DMA((sent,)))
    room.append(pltpu.SemaphoreType.DMA((len(far_in) + len(far_out) + blocks,)))
    return pl.pallas_call(
        wrapped,
        out_shape=[jax.ShapeDtypeStruct(shape, kind) for shape, kind in shapes],
        in_specs=[pl.BlockSpec(memory_space=pltpu.SMEM)] * scalars
        + [any_space] * blocks
        + [vmem] * near_in
        + [any_space] * len(far_in),
        out_specs=[vmem] * (near_out - sent) + [hbm] * (len(far_out) + sent),
        scratch_shapes=room,
        compiler_params=pltpu.CompilerParams(vmem_limit_bytes=grant << 20),
        cost_estimate=pl.CostEstimate(flops=flops, bytes_accessed=moved, transcendentals=0),
    )(*args)


def dot(a, b, **kw):
    return jnp.dot(a, b, preferred_element_type=F32, **kw)


def iota(shape, dim):
    return lax.broadcasted_iota(jnp.int32, shape, dim)


def one_hot(rows, columns, width, wrap):
    return ((iota((rows, columns), 0) & (wrap - 1)) == iota((rows, columns), 1) // width).astype(BF16)


def spread(x, head_of):
    hi = x.astype(BF16)
    return dot(hi, head_of) + dot((x - hi.astype(F32)).astype(BF16), head_of)


def prompt_start(lengths_ref, positions):
    start, end = jnp.zeros_like(positions), 0
    for i in range(lengths_ref.shape[0]):
        end = end + lengths_ref[i]
        start = jnp.maximum(start, jnp.where(positions >= end, end, 0))
    return start


def lanes(row):
    return jnp.pad(row, ((0, 0), (0, -row.shape[1] % 128)))


def silu(x):
    return x / (1.0 + jnp.exp(-x))


def convolve(rows_ref, at, taps, positions, start):
    tokens, width = positions.shape[0], taps.shape[0]
    total = jnp.zeros(positions.shape, F32)
    for k in range(width):
        back = width - 1 - k
        rows = rows_ref[EDGE - back : EDGE - back + tokens, at : at + positions.shape[1]]
        total = total + jnp.where(positions - back >= start, taps[k : k + 1] * rows, 0.0)
    return silu(total).astype(BF16)


def fetch(blocks, held, sems, columns, order=None):
    depth = blocks[0].shape[0]
    copies = []
    for i, k in enumerate(order or range(len(blocks))):
        copy = pltpu.make_async_copy(
            blocks[k].at[:, columns], held.at[i * depth : (i + 1) * depth], sems.at[i]
        )
        copy.start()
        copies.append(copy)
    return copies


def arrange_body(block_rows, by_arrival, ready, sems, at_ref, order_ref, *refs):
    *pieces, edge_ref, h_ref, held = refs
    x_at, core_at, tp_at = at_ref[0], at_ref[1], at_ref[2]
    tokens, features = pieces[0].shape
    x_size, z_size, core_size = SIZES
    ready()
    for d, piece in enumerate(pieces):
        held[:tokens, d * features : (d + 1) * features] = piece[...]
    held[tokens:] = edge_ref[...]
    wide = h_ref.shape[1]
    each = features // block_rows
    lane = iota((8, wide), 1)
    block = lane // block_rows
    source = lane - block * block_rows
    if by_arrival:
        chips = [
            ((x_at + x_size - d) & (x_size - 1)) * z_size + z
            for d in range(x_size)
            for z in range(z_size)
        ]
        stored = [chip * core_size + (core_at ^ turn) for turn in range(core_size) for chip in chips]
    else:
        stored = range(x_size * z_size * core_size)
    for count, at in enumerate(stored):
        model = order_ref[at]
        piece = (tp_at + len(pieces) - model // each) & (len(pieces) - 1)
        base = (piece * each + (model & (each - 1))) * block_rows
        source = source + jnp.where(block == count, base, 0)
    for at in range(0, wide, 256):
        total = jnp.zeros((h_ref.shape[0], 256), F32)
        for k in range(0, wide, features):
            match = iota((features, 256), 0) + k == source[:1, at : at + 256]
            total = total + dot(held[:, k : k + features], match.astype(F32).astype(BF16))
        h_ref[:, at : at + 256] = total.astype(BF16)


def early_body(head_dim, ready, sems, first_ref, lengths_ref, *refs):
    *blocks, h_ref, conv_value, conv_shared, bias, a_log = refs[:-8]
    x_ref, b_ref, dt_ref, cum_ref, sent_ref, held, rows, lines = refs[-8:]
    tokens, inner = x_ref.shape
    copies = fetch(blocks, held, sems, slice(0, held.shape[1]))
    ready()
    half, middle = len(blocks) // 2, held.shape[0] // 2
    for copy in copies[:half]:
        copy.wait()
    for at in range(0, held.shape[1], 256):
        rows[:, at : at + 256] = dot(h_ref[:, :middle], held[:middle, at : at + 256])
    for copy in copies[half:]:
        copy.wait()
    for at in range(0, held.shape[1], 256):
        part = rows[:, at : at + 256] + dot(h_ref[:, middle:], held[middle:, at : at + 256])
        part = part.astype(BF16).astype(F32)
        rows[EDGE:, at : at + 256] = part[:tokens]
        rows[:EDGE, at : at + 256] = part[tokens:]
    first = first_ref[0]
    positions = first + iota((tokens, 128), 0)
    start = prompt_start(lengths_ref, positions)
    last_start = prompt_start(lengths_ref, first + tokens - 1)
    for at in range(0, inner, 128):
        x_ref[:, at : at + 128] = convolve(
            rows, at, conv_value[:, at : at + 128], positions, start
        )
    b_half = convolve(rows, inner, conv_shared[:, :128], positions, start)
    b_ref[...] = b_half
    raw = rows[EDGE:, inner + 128 :] + lanes(bias[...])
    dt = jnp.maximum(raw, 0.0) + jnp.log1p(jnp.exp(-jnp.abs(raw)))
    below = (iota((tokens, tokens), 0) >= iota((tokens, tokens), 1)).astype(F32)
    cum = dot(below, -dt * jnp.exp(lanes(a_log[...])), precision=lax.Precision.HIGHEST)
    dt_ref[...] = dt
    cum_ref[...] = cum
    last = cum[tokens - 1 :]
    tail = jnp.where(positions >= last_start, jnp.exp(last - cum), 0.0) * dt
    head_of = one_hot(128, inner, head_dim, 128)
    weighted = (spread(tail, head_of) * x_ref[...].astype(F32)).astype(BF16)
    fresh = dot(b_half.astype(F32).T.astype(BF16), weighted)
    lines[...] = jnp.zeros_like(lines)
    count = lines.shape[0] // LINES
    line = 0
    for row in range(0, fresh.shape[0], count):
        for at in range(0, inner, 128):
            lines[pl.ds(line, count, stride=LINES), :] = fresh[row : row + count, at : at + 128]
            line += 1
    keep = jnp.where(last_start < first, jnp.exp(last), 0.0)
    keep = jnp.broadcast_to(keep, (8, 128))
    keep_hi = keep.astype(BF16).astype(F32)
    keep_lo = pltpu.roll(keep - keep_hi, 64, axis=1)
    both = jnp.where(iota((8, 128), 1) < 64, keep_hi, keep_lo)
    lines[pl.ds(line, count, stride=LINES), :] = jnp.concatenate([both] * (count // 8), axis=0)
    sent_ref[...] = lines[...].astype(BF16)


def scan_body(head_dim, inner, copies, ready, sems, sent_ref, out_ref, lines):
    ready()
    lines[...] = sent_ref[...].astype(F32)
    count = lines.shape[0] // LINES
    tiles = inner // 128

    def line(r):
        return lines[pl.ds(r, count, stride=LINES), :]

    keeps = line(copies * tiles).astype(BF16)
    row = iota((count, 128), 0)

    def down(x, d):
        return jnp.where(row >= d, pltpu.roll(x, d, axis=0), 0.0)

    head_of = one_hot(128, inner, head_dim, 64)
    for t in range(tiles):
        keep = dot(keeps, head_of[:, t * 128 : (t + 1) * 128])
        states = [line(i * tiles + t) for i in range(copies)]
        d = 1
        while d < count:
            states = [x + keep * down(x, d) for x in states]
            keep = keep * down(keep, d)
            d *= 2
        for i, x in enumerate(states):
            lines[pl.ds(i * tiles + t, count, stride=LINES), :] = down(x, 1)
    out_ref[...] = lines[...].astype(BF16)


def middle_body(head_dim, ready, sems, first_ref, lengths_ref, *refs):
    late_ref, h_ref, conv_shared, x_ref, b_ref, dt_ref, cum_ref, skip = refs[:-6]
    direct_ref, carry_ref, c_ref, held, c_rows, gate = refs[-6:]
    tokens, inner = x_ref.shape
    copy = pltpu.make_async_copy(late_ref.at[:, : held.shape[1]], held, sems.at[0])
    copy.start()
    ready()
    copy.wait()
    for at in range(0, inner, 256):
        g = dot(h_ref[:tokens], held[:, at : at + 256])
        gate[:, at : at + 256] = silu(g.astype(BF16).astype(F32))
    part = dot(h_ref[...], held[:, inner:]).astype(BF16).astype(F32)
    c_rows[EDGE:] = part[:tokens]
    c_rows[:EDGE] = part[tokens:]
    first = first_ref[0]
    positions = first + iota((tokens, 128), 0)
    start = prompt_start(lengths_ref, positions)
    c_half = convolve(c_rows, 0, conv_shared[:, 128:], positions, start)
    c_ref[...] = c_half
    scores = lax.dot_general(
        c_half, b_ref[...], (((1,), (1,)), ((), ())), preferred_element_type=F32
    )
    i, j = iota((tokens, tokens), 0), iota((tokens, tokens), 1)
    start_wide = jnp.concatenate([start] * (tokens // 128), axis=1)
    scores = jnp.where((j <= i) & (first + j >= start_wide), scores, 0.0)
    dt, cum = dt_ref[...], cum_ref[...]
    head_of = one_hot(128, inner, head_dim, 128)
    stepped = (spread(dt, head_of) * x_ref[...].astype(F32)).astype(BF16)
    cum_t = cum.T
    carry = jnp.where(start < first, jnp.exp(cum), 0.0)
    carry_ref[...] = (spread(carry, head_of) * gate[...]).astype(BF16)
    each = 128 // head_dim
    for at in range(0, inner, 128):
        sums = []
        for h in range(at // head_dim, at // head_dim + each):
            gaps = jnp.minimum(cum[:, h : h + 1] - cum_t[h : h + 1, :], 0.0)
            weights = (jnp.exp(gaps) * scores).astype(BF16)
            sums.append(dot(weights, stepped[:, h * head_dim : (h + 1) * head_dim]))
        cut = slice(at, at + 128)
        direct = jnp.concatenate(sums, axis=1) + skip[:, cut] * x_ref[:, cut].astype(F32)
        direct_ref[:, cut] = (direct * gate[:, cut]).astype(BF16)


def last_body(ready, sems, turn_ref, late_ref, *refs):
    carried_ref, direct_ref, carry_ref, c_ref, gain = refs[:5]
    *outs, held, lines, shares, out_w, leaving = refs[5:]
    tokens, inner = direct_ref.shape
    wide = late_ref.shape[1]
    copy = pltpu.make_async_copy(late_ref.at[:, wide - inner :], out_w, sems.at[0])
    copy.start()
    ready()
    lines[...] = carried_ref[...].astype(F32)
    count = lines.shape[0] // LINES
    line = 0
    for row in range(0, held.shape[0], count):
        for at in range(0, inner, 128):
            cut = lines[pl.ds(line, count, stride=LINES), :]
            held[row : row + count, at : at + 128] = cut.astype(BF16)
            line += 1
    direct, carry = direct_ref[...].astype(F32), carry_ref[...].astype(F32)
    gated = direct + carry * dot(c_ref[...], held[...])
    scaled = (gated * gain[...]).astype(BF16)
    nt = (((1,), (1,)), ((), ()))
    features = shares.shape[2]
    squares = lax.dot_general(
        jnp.ones((8, inner), F32),
        gated * gated,
        nt,
        precision=lax.Precision.HIGHEST,
        preferred_element_type=F32,
    )
    hi = squares.astype(BF16).astype(F32)
    row = iota(squares.shape, 0)
    riding = jnp.where(row == 0, hi, jnp.where(row == 1, squares - hi, 0.0)).astype(BF16)
    copy.wait()
    copies = []
    for d in list(range(1, len(outs))) + [0]:
        at = pl.multiple_of(((turn_ref[0] + d) & (len(outs) - 1)) * features, features)
        rows = out_w[pl.ds(at, features), :]
        product = lax.dot_general(scaled, rows, nt, preferred_element_type=F32)
        shares[d, :tokens] = product.astype(BF16)
        shares[d, tokens:, :tokens] = riding
        shares[d, tokens:, tokens:] = jnp.zeros((8, features - tokens), BF16)
        copies.append(pltpu.make_async_copy(shares.at[d], outs[d], leaving.at[d]))
        copies[-1].start()
    for copy in copies:
        copy.wait()


def on_device(
    hidden_in,
    w_in_gate,
    w_in_value,
    w_in_shared,
    w_in_step,
    conv_value,
    conv_shared,
    dt_bias,
    a_log,
    skip_gain,
    norm_gain,
    w_out,
    prompt_lengths,
    row_blocks,
):
    x_size, z_size, core_size = SIZES
    seq_count = x_size * z_size * core_size
    tp_count = lax.axis_size("tp")
    tokens, features = hidden_in.shape
    rows_here, inner = w_in_value.shape
    shared = w_in_shared.shape[1]
    heads = dt_bias.shape[0]
    head_dim = inner // heads
    state = shared // 2
    x_at, z_at, core_at = (lax.axis_index(name) for name in SEQ)
    tp_at = lax.axis_index("tp")
    seq_at = (x_at * z_size + z_at) * core_size + core_at

    x_shifts = list(range(1, x_size))

    def x_all(block):
        return [block] + [ahead(block, "x", d) for d in x_shifts]

    tie = lax.optimization_barrier

    pieces = [hidden_in] + [ahead(hidden_in, "tp", d) for d in range(1, tp_count)]
    early_width = inner + state + heads + -heads % 128
    early = pack(pack_body, early_width, w_in_value, w_in_shared, w_in_step.T)
    late = pack(pack_late_body, 2 * inner + state, w_in_gate, w_in_shared, w_out.T)
    late = lax.all_gather(late, SEQ, axis=0, tiled=True)
    own = x_all(lax.all_gather(early, "z", axis=0, tiled=True))
    edge = jnp.concatenate([piece[tokens - EDGE :] for piece in pieces], axis=1)
    edge = lax.ppermute(edge, SEQ, [(i, i + 1) for i in range(seq_count - 1)])
    rows, model_width = tokens + EDGE, features * tp_count
    places = jnp.stack([x_at, core_at, tp_at])

    def arrange(by_arrival, pieces):
        return call(
            functools.partial(arrange_body, rows_here, by_arrival),
            [((rows, model_width), BF16)],
            [places, row_blocks] + pieces + [edge],
            scalars=2,
            scratch=[((rows, model_width), BF16)],
            flops=2 * rows * model_width * model_width,
            grant=40,
        )[0]

    h = arrange(True, pieces)
    own[-1], h = tie((own[-1], h))
    other = [ahead(block, "core", 1) for block in own]

    first = jnp.reshape(seq_at * tokens, (1,))
    copies = state // seq_count
    x_rows, b_half, steps, cumulative, sent = call(
        functools.partial(early_body, head_dim),
        [
            ((tokens, inner), BF16),
            ((tokens, state), BF16),
            ((tokens, 128), F32),
            ((tokens, 128), F32),
            ((seq_count * LINES, 128), BF16),
        ],
        [first, prompt_lengths] + own + other + [h, conv_value, conv_shared, dt_bias[None], a_log[None]],
        scalars=2,
        blocks=len(own + other),
        grant=40,
        scratch=[
            ((model_width, early_width), BF16),
            ((rows, early_width), F32),
            ((seq_count * LINES, 128), F32),
        ],
        flops=2 * rows * model_width * early_width,
    )
    received = lax.all_to_all(sent.reshape(seq_count, LINES, 128), SEQ, 0, 0, tiled=True)
    (scanned,) = call(
        functools.partial(scan_body, head_dim, inner, copies),
        [((seq_count * LINES, 128), BF16)],
        [received.reshape(seq_count * LINES, 128)],
        near_in=1,
        grant=40,
        scratch=[((seq_count * LINES, 128), F32)],
    )
    carried = lax.all_to_all(scanned.reshape(seq_count, LINES, 128), SEQ, 0, 0, tiled=True)
    carried = carried.reshape(seq_count * LINES, 128)
    pieces, _ = tie((pieces, sent))
    h_late = arrange(False, pieces)
    direct, carry, c_half = call(
        functools.partial(middle_body, head_dim),
        [
            ((tokens, inner), BF16),
            ((tokens, inner), BF16),
            ((tokens, state), BF16),
        ],
        [first, prompt_lengths, late]
        + [h_late, conv_shared, x_rows, b_half, steps, cumulative, jnp.repeat(skip_gain, head_dim)[None]],
        scalars=2,
        blocks=1,
        scratch=[
            ((model_width, inner + state), BF16),
            ((rows, state), F32),
            ((tokens, inner), F32),
        ],
        flops=2 * rows * model_width * (inner + state),
    )
    shares = call(
        last_body,
        [((tokens + 8, features), BF16)] * tp_count,
        [
            jnp.reshape(tp_at, (1,)),
            late,
            carried,
            direct,
            carry,
            c_half,
            norm_gain[None],
        ],
        scalars=1,
        blocks=1,
        scratch=[
            ((state, inner), BF16),
            ((seq_count * LINES, 128), F32),
            ((tp_count, tokens + 8, features), BF16),
            ((model_width, inner), BF16),
        ],
        sent=tp_count,
        flops=2 * tokens * inner * model_width,
    )
    parts = [shares[0]] + [ahead(shares[d], "tp", d) for d in range(1, tp_count)]
    summed = sum(part.astype(F32) for part in parts)
    total = summed[tokens, :tokens] + summed[tokens + 1, :tokens]
    scale = lax.rsqrt(total / (inner * tp_count) + EPSILON)
    return (summed[:tokens] * scale[:, None]).astype(BF16)


def solution(mesh):
    fine = Mesh(mesh.devices.reshape(SIZES + (-1,)), SEQ + ("tp",))
    return jax.shard_map(
        on_device,
        mesh=fine,
        in_specs=(
            P(SEQ, "tp"),
            P(SEQ, "tp"),
            P(SEQ, "tp"),
            P(SEQ, None),
            P(SEQ, "tp"),
            P(None, "tp"),
            P(),
            P("tp"),
            P("tp"),
            P("tp"),
            P("tp"),
            P("tp", SEQ),
            P(),
            P(),
        ),
        out_specs=P(SEQ, "tp"),
        check_vma=False,
    )
```

```python
import functools

import jax
import jax.numpy as jnp
from jax import lax
from jax.experimental import pallas as pl
from jax.experimental.pallas import tpu as pltpu
from jax.sharding import Mesh, PartitionSpec as P

EPSILON = 1e-05
EDGE = 8
LINES = 16
SEQ = ("x", "z", "core")
SIZES = (4, 8, 2)
BF16 = jnp.bfloat16
F32 = jnp.float32


def ahead(block, axis, distance):
    count = lax.axis_size(axis)
    return lax.ppermute(block, axis, [(i, (i + distance) % count) for i in range(count)])


def pack_body(value_ref, shared_ref, step_ref, gate_ref, out_t_ref, out_ref):
    inner, half, heads = value_ref.shape[1], shared_ref.shape[1] // 2, step_ref.shape[0]
    rest = -heads % 128
    step = jnp.pad(step_ref[...].T, ((0, 0), (0, rest)))
    at = 0
    for piece in (
        value_ref[...],
        shared_ref[:, :half],
        step,
        gate_ref[...],
        shared_ref[:, half:],
        out_t_ref[...],
    ):
        out_ref[:, at : at + piece.shape[1]] = piece.astype(BF16)
        at += piece.shape[1]


def pack(value, shared, step, gate, out_t):
    rows, inner = value.shape
    heads = step.shape[1]
    width = 3 * inner + shared.shape[1] + heads + -heads % 128
    return pl.pallas_call(
        pack_body,
        out_shape=jax.ShapeDtypeStruct((rows, width), BF16),
        in_specs=[pl.BlockSpec(memory_space=pltpu.VMEM)] * 5,
        out_specs=pl.BlockSpec(memory_space=pltpu.VMEM),
    )(value, shared, step.T, gate, out_t)


def call(
    body, shapes, args, scalars=0, blocks=0, near_in=0, near_out=0, sent=0, scratch=(), flops=0, grant=60
):
    hbm, vmem = pl.BlockSpec(memory_space=pltpu.HBM), pl.BlockSpec(memory_space=pltpu.VMEM)
    fixed = scalars + blocks + near_in
    near_out = near_out + sent
    far_in, far_out = args[fixed:], shapes[near_out:]
    moved = sum(x.size * x.dtype.itemsize for x in args)

    def wrapped(*refs):
        ins, rest = refs[: len(args)], refs[len(args) :]
        outs, rest = rest[: len(shapes)], rest[len(shapes) :]
        held_in, rest = rest[: len(far_in)], rest[len(far_in) :]
        held_out, rest = rest[: len(far_out)], rest[len(far_out) :]
        *room, sems = rest
        copies = [
            pltpu.make_async_copy(src, dst, sems.at[i])
            for i, (src, dst) in enumerate(zip(ins[fixed:], held_in))
        ]
        for copy in copies:
            copy.start()
        free = sems.at[pl.ds(len(far_in) + len(far_out), blocks)] if blocks else None

        def ready():
            for copy in copies:
                copy.wait()

        body(ready, free, *ins[:fixed], *held_in, *outs[:near_out], *held_out, *room)
        copies_out = [
            pltpu.make_async_copy(src, dst, sems.at[len(far_in) + i])
            for i, (src, dst) in enumerate(zip(held_out, outs[near_out:]))
        ]
        for copy in copies_out:
            copy.start()
        for copy in copies_out:
            copy.wait()

    room = [pltpu.VMEM(x.shape, x.dtype) for x in far_in]
    room += [pltpu.VMEM(shape, kind) for shape, kind in far_out]
    room += [pltpu.VMEM(shape, kind) for shape, kind in scratch]
    if sent:
        room.append(pltpu.SemaphoreType.DMA((sent,)))
    room.append(pltpu.SemaphoreType.DMA((len(far_in) + len(far_out) + blocks,)))
    return pl.pallas_call(
        wrapped,
        out_shape=[jax.ShapeDtypeStruct(shape, kind) for shape, kind in shapes],
        in_specs=[pl.BlockSpec(memory_space=pltpu.SMEM)] * scalars
        + [hbm] * blocks
        + [vmem] * near_in
        + [hbm] * len(far_in),
        out_specs=[vmem] * (near_out - sent) + [hbm] * (len(far_out) + sent),
        scratch_shapes=room,
        compiler_params=pltpu.CompilerParams(vmem_limit_bytes=grant << 20),
        cost_estimate=pl.CostEstimate(flops=flops, bytes_accessed=moved, transcendentals=0),
    )(*args)


def dot(a, b, **kw):
    return jnp.dot(a, b, preferred_element_type=F32, **kw)


def iota(shape, dim):
    return lax.broadcasted_iota(jnp.int32, shape, dim)


def one_hot(rows, columns, width, wrap):
    return ((iota((rows, columns), 0) & (wrap - 1)) == iota((rows, columns), 1) // width).astype(BF16)


def spread(x, head_of):
    hi = x.astype(BF16)
    return dot(hi, head_of) + dot((x - hi.astype(F32)).astype(BF16), head_of)


def prompt_start(lengths_ref, positions):
    start, end = jnp.zeros_like(positions), 0
    for i in range(lengths_ref.shape[0]):
        end = end + lengths_ref[i]
        start = jnp.maximum(start, jnp.where(positions >= end, end, 0))
    return start


def lanes(row):
    return jnp.pad(row, ((0, 0), (0, -row.shape[1] % 128)))


def silu(x):
    return x / (1.0 + jnp.exp(-x))


def convolve(rows_ref, at, taps, positions, start):
    tokens, width = positions.shape[0], taps.shape[0]
    total = jnp.zeros(positions.shape, F32)
    for k in range(width):
        back = width - 1 - k
        rows = rows_ref[EDGE - back : EDGE - back + tokens, at : at + positions.shape[1]]
        total = total + jnp.where(positions - back >= start, taps[k : k + 1] * rows, 0.0)
    return silu(total).astype(BF16)


def fetch(blocks, held, sems, columns, order=None):
    depth = blocks[0].shape[0]
    copies = []
    for i, k in enumerate(order or range(len(blocks))):
        copy = pltpu.make_async_copy(
            blocks[k].at[:, columns], held.at[i * depth : (i + 1) * depth], sems.at[i]
        )
        copy.start()
        copies.append(copy)
    return copies


def arrange_body(block_rows, ready, sems, at_ref, order_ref, *refs):
    *pieces, edge_ref, h_ref, held = refs
    ready()
    x_at, core_at, tp_at = at_ref[0], at_ref[1], at_ref[2]
    tokens, features = pieces[0].shape
    x_size, z_size, core_size = SIZES
    for d, piece in enumerate(pieces):
        held[:tokens, d * features : (d + 1) * features] = piece[...]
    held[tokens:] = edge_ref[...]
    wide = h_ref.shape[1]
    each = features // block_rows
    lane = iota((8, wide), 1)
    block = lane // block_rows
    source = lane - block * block_rows
    count = 0
    for turn in range(core_size):
        for d in range(x_size):
            chip = ((x_at + x_size - d) & (x_size - 1)) * z_size
            for z in range(z_size):
                model = order_ref[(chip + z) * core_size + (core_at ^ turn)]
                piece = (tp_at + len(pieces) - model // each) & (len(pieces) - 1)
                base = (piece * each + (model & (each - 1))) * block_rows
                source = source + jnp.where(block == count, base, 0)
                count += 1
    for at in range(0, wide, 256):
        total = jnp.zeros((h_ref.shape[0], 256), F32)
        for k in range(0, wide, features):
            match = iota((features, 256), 0) + k == source[:1, at : at + 256]
            total = total + dot(held[:, k : k + features], match.astype(F32).astype(BF16))
        h_ref[:, at : at + 256] = total.astype(BF16)


def early_body(head_dim, ready, sems, first_ref, lengths_ref, *refs):
    *blocks, h_ref, conv_value, conv_shared, bias, a_log = refs[:-8]
    x_ref, b_ref, dt_ref, cum_ref, sent_ref, held, rows, lines = refs[-8:]
    tokens, inner = x_ref.shape
    copies = fetch(blocks, held, sems, slice(0, held.shape[1]))
    ready()
    half, middle = len(blocks) // 2, held.shape[0] // 2
    for copy in copies[:half]:
        copy.wait()
    for at in range(0, held.shape[1], 256):
        rows[:, at : at + 256] = dot(h_ref[:, :middle], held[:middle, at : at + 256])
    for copy in copies[half:]:
        copy.wait()
    for at in range(0, held.shape[1], 256):
        part = rows[:, at : at + 256] + dot(h_ref[:, middle:], held[middle:, at : at + 256])
        part = part.astype(BF16).astype(F32)
        rows[EDGE:, at : at + 256] = part[:tokens]
        rows[:EDGE, at : at + 256] = part[tokens:]
    first = first_ref[0]
    positions = first + iota((tokens, 128), 0)
    start = prompt_start(lengths_ref, positions)
    last_start = prompt_start(lengths_ref, first + tokens - 1)
    for at in range(0, inner, 128):
        x_ref[:, at : at + 128] = convolve(
            rows, at, conv_value[:, at : at + 128], positions, start
        )
    b_half = convolve(rows, inner, conv_shared[:, :128], positions, start)
    b_ref[...] = b_half
    raw = rows[EDGE:, inner + 128 :] + lanes(bias[...])
    dt = jnp.maximum(raw, 0.0) + jnp.log1p(jnp.exp(-jnp.abs(raw)))
    below = (iota((tokens, tokens), 0) >= iota((tokens, tokens), 1)).astype(F32)
    cum = dot(below, -dt * jnp.exp(lanes(a_log[...])), precision=lax.Precision.HIGHEST)
    dt_ref[...] = dt
    cum_ref[...] = cum
    last = cum[tokens - 1 :]
    tail = jnp.where(positions >= last_start, jnp.exp(last - cum), 0.0) * dt
    head_of = one_hot(128, inner, head_dim, 128)
    weighted = (spread(tail, head_of) * x_ref[...].astype(F32)).astype(BF16)
    fresh = dot(b_half.astype(F32).T.astype(BF16), weighted)
    lines[...] = jnp.zeros_like(lines)
    count = lines.shape[0] // LINES
    line = 0
    for row in range(0, fresh.shape[0], count):
        for at in range(0, inner, 128):
            lines[pl.ds(line, count, stride=LINES), :] = fresh[row : row + count, at : at + 128]
            line += 1
    keep = jnp.where(last_start < first, jnp.exp(last), 0.0)
    keep = jnp.broadcast_to(keep, (8, 128))
    keep_hi = keep.astype(BF16).astype(F32)
    keep_lo = pltpu.roll(keep - keep_hi, 64, axis=1)
    both = jnp.where(iota((8, 128), 1) < 64, keep_hi, keep_lo)
    lines[pl.ds(line, count, stride=LINES), :] = jnp.concatenate([both] * (count // 8), axis=0)
    sent_ref[...] = lines[...].astype(BF16)


def scan_body(head_dim, inner, copies, ready, sems, sent_ref, out_ref, lines):
    ready()
    lines[...] = sent_ref[...].astype(F32)
    count = lines.shape[0] // LINES
    tiles = inner // 128

    def line(r):
        return lines[pl.ds(r, count, stride=LINES), :]

    keeps = line(copies * tiles).astype(BF16)
    row = iota((count, 128), 0)

    def down(x, d):
        return jnp.where(row >= d, pltpu.roll(x, d, axis=0), 0.0)

    head_of = one_hot(128, inner, head_dim, 64)
    for t in range(tiles):
        keep = dot(keeps, head_of[:, t * 128 : (t + 1) * 128])
        states = [line(i * tiles + t) for i in range(copies)]
        d = 1
        while d < count:
            states = [x + keep * down(x, d) for x in states]
            keep = keep * down(keep, d)
            d *= 2
        for i, x in enumerate(states):
            lines[pl.ds(i * tiles + t, count, stride=LINES), :] = down(x, 1)
    out_ref[...] = lines[...].astype(BF16)


def middle_body(head_dim, ready, sems, first_ref, lengths_ref, *refs):
    *blocks, h_ref, conv_shared, x_ref, b_ref, dt_ref, cum_ref, skip = refs[:-6]
    direct_ref, carry_ref, c_ref, held, c_rows, gate = refs[-6:]
    tokens, inner = x_ref.shape
    wide = held.shape[1]
    copies = fetch(blocks, held, sems, slice(0, wide))
    ready()
    for copy in copies:
        copy.wait()
    for at in range(0, inner, 256):
        g = dot(h_ref[:tokens], held[:, at : at + 256])
        gate[:, at : at + 256] = silu(g.astype(BF16).astype(F32))
    part = dot(h_ref[...], held[:, inner:]).astype(BF16).astype(F32)
    c_rows[EDGE:] = part[:tokens]
    c_rows[:EDGE] = part[tokens:]
    first = first_ref[0]
    positions = first + iota((tokens, 128), 0)
    start = prompt_start(lengths_ref, positions)
    c_half = convolve(c_rows, 0, conv_shared[:, 128:], positions, start)
    c_ref[...] = c_half
    scores = lax.dot_general(
        c_half, b_ref[...], (((1,), (1,)), ((), ())), preferred_element_type=F32
    )
    i, j = iota((tokens, tokens), 0), iota((tokens, tokens), 1)
    start_wide = jnp.concatenate([start] * (tokens // 128), axis=1)
    scores = jnp.where((j <= i) & (first + j >= start_wide), scores, 0.0)
    dt, cum = dt_ref[...], cum_ref[...]
    head_of = one_hot(128, inner, head_dim, 128)
    stepped = (spread(dt, head_of) * x_ref[...].astype(F32)).astype(BF16)
    cum_t = cum.T
    carry = jnp.where(start < first, jnp.exp(cum), 0.0)
    carry_ref[...] = (spread(carry, head_of) * gate[...]).astype(BF16)
    each = 128 // head_dim
    for at in range(0, inner, 128):
        sums = []
        for h in range(at // head_dim, at // head_dim + each):
            gaps = jnp.minimum(cum[:, h : h + 1] - cum_t[h : h + 1, :], 0.0)
            weights = (jnp.exp(gaps) * scores).astype(BF16)
            sums.append(dot(weights, stepped[:, h * head_dim : (h + 1) * head_dim]))
        cut = slice(at, at + 128)
        direct = jnp.concatenate(sums, axis=1) + skip[:, cut] * x_ref[:, cut].astype(F32)
        direct_ref[:, cut] = (direct * gate[:, cut]).astype(BF16)


def last_body(ready, sems, turn_ref, *refs):
    *blocks, carried_ref, direct_ref, carry_ref, c_ref, gain = refs[:-9]
    *outs, held, lines, shares, out_w, leaving = refs[-9:]
    half, wide, inner = len(blocks) // 2, blocks[0].shape[2], out_w.shape[4]
    copies = []
    for i, block in enumerate(blocks):
        copy = pltpu.make_async_copy(
            block.at[:, :, wide - inner :],
            out_w.at[i % half, :, turn_ref[1] ^ (i // half)],
            sems.at[i],
        )
        copy.start()
        copies.append(copy)
    ready()
    tokens, inner = direct_ref.shape
    lines[...] = carried_ref[...].astype(F32)
    count = lines.shape[0] // LINES
    line = 0
    for row in range(0, held.shape[0], count):
        for at in range(0, inner, 128):
            cut = lines[pl.ds(line, count, stride=LINES), :]
            held[row : row + count, at : at + 128] = cut.astype(BF16)
            line += 1
    direct, carry = direct_ref[...].astype(F32), carry_ref[...].astype(F32)
    gated = direct + carry * dot(c_ref[...], held[...])
    scaled = (gated * gain[...]).astype(BF16)
    nt = (((1,), (1,)), ((), ()))
    features = shares.shape[2]
    squares = lax.dot_general(
        jnp.ones((8, inner), F32),
        gated * gated,
        nt,
        precision=lax.Precision.HIGHEST,
        preferred_element_type=F32,
    )
    hi = squares.astype(BF16).astype(F32)
    row = iota(squares.shape, 0)
    riding = jnp.where(row == 0, hi, jnp.where(row == 1, squares - hi, 0.0)).astype(BF16)
    for copy in copies:
        copy.wait()
    copies = []
    for d in list(range(1, len(outs))) + [0]:
        rows = out_w[(turn_ref[0] + len(outs) - d) & (len(outs) - 1)].reshape(features, inner)
        product = lax.dot_general(scaled, rows, nt, preferred_element_type=F32)
        shares[d, :tokens] = product.astype(BF16)
        shares[d, tokens:, :tokens] = riding
        shares[d, tokens:, tokens:] = jnp.zeros((8, features - tokens), BF16)
        copies.append(pltpu.make_async_copy(shares.at[d], outs[d], leaving.at[d]))
        copies[-1].start()
    for copy in copies:
        copy.wait()


def on_device(
    hidden_in,
    w_in_gate,
    w_in_value,
    w_in_shared,
    w_in_step,
    conv_value,
    conv_shared,
    dt_bias,
    a_log,
    skip_gain,
    norm_gain,
    w_out,
    prompt_lengths,
    row_blocks,
):
    x_size, z_size, core_size = SIZES
    seq_count = x_size * z_size * core_size
    tp_count = lax.axis_size("tp")
    tokens, features = hidden_in.shape
    rows_here, inner = w_in_value.shape
    shared = w_in_shared.shape[1]
    heads = dt_bias.shape[0]
    head_dim = inner // heads
    state = shared // 2
    x_at, z_at, core_at = (lax.axis_index(name) for name in SEQ)
    tp_at = lax.axis_index("tp")
    seq_at = (x_at * z_size + z_at) * core_size + core_at

    x_shifts = list(range(1, x_size))

    def x_all(block):
        return [block] + [ahead(block, "x", d) for d in x_shifts]

    tie = lax.optimization_barrier

    pieces = [hidden_in] + [ahead(hidden_in, "tp", d) for d in range(1, tp_count)]
    packed = pack(w_in_value, w_in_shared, w_in_step, w_in_gate, w_out.T)
    along_z = lax.all_gather(packed, "z", axis=0, tiled=True)
    early_width = packed.shape[1] - 2 * inner - state
    own = x_all(along_z[:, :early_width])
    late = along_z[:, early_width:]
    edge = jnp.concatenate([piece[tokens - EDGE :] for piece in pieces], axis=1)
    edge = lax.ppermute(edge, SEQ, [(i, i + 1) for i in range(seq_count - 1)])
    rows, model_width = tokens + EDGE, features * tp_count
    (h,) = call(
        functools.partial(arrange_body, rows_here),
        [((rows, model_width), BF16)],
        [jnp.stack([x_at, core_at, tp_at]), row_blocks] + pieces + [edge],
        scalars=2,
        scratch=[((rows, model_width), BF16)],
        flops=2 * rows * model_width * model_width,
    )
    own[-1], h, late = tie((own[-1], h, late))
    other = [ahead(block, "core", 1) for block in own]
    late_own = x_all(late)

    first = jnp.reshape(seq_at * tokens, (1,))
    copies = state // seq_count
    x_rows, b_half, steps, cumulative, sent = call(
        functools.partial(early_body, head_dim),
        [
            ((tokens, inner), BF16),
            ((tokens, state), BF16),
            ((tokens, 128), F32),
            ((tokens, 128), F32),
            ((seq_count * LINES, 128), BF16),
        ],
        [first, prompt_lengths] + own + other + [h, conv_value, conv_shared, dt_bias[None], a_log[None]],
        scalars=2,
        blocks=len(own + other),
        scratch=[
            ((model_width, early_width), BF16),
            ((rows, early_width), F32),
            ((seq_count * LINES, 128), F32),
        ],
        flops=2 * rows * model_width * early_width,
    )
    received = lax.all_to_all(sent.reshape(seq_count, LINES, 128), SEQ, 0, 0, tiled=True)
    (scanned,) = call(
        functools.partial(scan_body, head_dim, inner, copies),
        [((seq_count * LINES, 128), BF16)],
        [received.reshape(seq_count * LINES, 128)],
        near_in=1,
        grant=40,
        scratch=[((seq_count * LINES, 128), F32)],
    )
    carried = lax.all_to_all(scanned.reshape(seq_count, LINES, 128), SEQ, 0, 0, tiled=True)
    carried = carried.reshape(seq_count * LINES, 128)
    late_own, _ = tie((late_own, scanned))
    late_other = [ahead(block, "core", 1) for block in late_own]
    direct, carry, c_half = call(
        functools.partial(middle_body, head_dim),
        [
            ((tokens, inner), BF16),
            ((tokens, inner), BF16),
            ((tokens, state), BF16),
        ],
        [first, prompt_lengths]
        + late_own
        + late_other
        + [h, conv_shared, x_rows, b_half, steps, cumulative, jnp.repeat(skip_gain, head_dim)[None]],
        scalars=2,
        blocks=len(late_own + late_other),
        scratch=[
            ((model_width, inner + state), BF16),
            ((rows, state), F32),
            ((tokens, inner), F32),
        ],
        flops=2 * rows * model_width * (inner + state),
    )
    shares = call(
        last_body,
        [((tokens + 8, features), BF16)] * tp_count,
        [
            jnp.stack([x_at - tp_at + tp_count, core_at]),
            *[block.reshape(z_size, rows_here, -1) for block in late_own + late_other],
            carried,
            direct,
            carry,
            c_half,
            norm_gain[None],
        ],
        scalars=1,
        blocks=len(late_own + late_other),
        scratch=[
            ((state, inner), BF16),
            ((seq_count * LINES, 128), F32),
            ((tp_count, tokens + 8, features), BF16),
            ((x_size, z_size, core_size, rows_here, inner), BF16),
        ],
        sent=tp_count,
        flops=2 * tokens * inner * model_width,
    )
    parts = [shares[0]] + [ahead(shares[d], "tp", d) for d in range(1, tp_count)]
    total = sum(part[tokens : tokens + 2, :tokens].astype(F32) for part in parts)
    scale = lax.rsqrt((total[0] + total[1]) / (inner * tp_count) + EPSILON)
    scale = tie(scale)
    return (sum(part[:tokens].astype(F32) for part in parts) * scale[:, None]).astype(BF16)


def solution(mesh):
    fine = Mesh(mesh.devices.reshape(SIZES + (-1,)), SEQ + ("tp",))
    return jax.shard_map(
        on_device,
        mesh=fine,
        in_specs=(
            P(SEQ, "tp"),
            P(SEQ, "tp"),
            P(SEQ, "tp"),
            P(SEQ, None),
            P(SEQ, "tp"),
            P(None, "tp"),
            P(),
            P("tp"),
            P("tp"),
            P("tp"),
            P("tp"),
            P("tp", SEQ),
            P(),
            P(),
        ),
        out_specs=P(SEQ, "tp"),
        check_vma=False,
    )
```

```python
import functools

import jax
import jax.numpy as jnp
from jax import lax
from jax.experimental import pallas as pl
from jax.experimental.pallas import tpu as pltpu
from jax.sharding import Mesh, PartitionSpec as P

EPSILON = 1e-05
EDGE = 8
LINES = 16
SEQ = ("x", "z", "core")
SIZES = (4, 8, 2)
BF16 = jnp.bfloat16
F32 = jnp.float32


def ahead(block, axis, distance):
    count = lax.axis_size(axis)
    return lax.ppermute(block, axis, [(i, (i + distance) % count) for i in range(count)])


def pack_body(value_ref, shared_ref, step_ref, gate_ref, out_t_ref, out_ref):
    inner, half, heads = value_ref.shape[1], shared_ref.shape[1] // 2, step_ref.shape[0]
    rest = -heads % 128
    step = jnp.pad(step_ref[...].T, ((0, 0), (0, rest)))
    at = 0
    for piece in (
        value_ref[...],
        shared_ref[:, :half],
        step,
        gate_ref[...],
        shared_ref[:, half:],
        out_t_ref[...],
    ):
        out_ref[:, at : at + piece.shape[1]] = piece.astype(BF16)
        at += piece.shape[1]


def pack(value, shared, step, gate, out_t):
    rows, inner = value.shape
    heads = step.shape[1]
    width = 3 * inner + shared.shape[1] + heads + -heads % 128
    return pl.pallas_call(
        pack_body,
        out_shape=jax.ShapeDtypeStruct((rows, width), BF16),
        in_specs=[pl.BlockSpec(memory_space=pltpu.VMEM)] * 5,
        out_specs=pl.BlockSpec(memory_space=pltpu.VMEM),
    )(value, shared, step.T, gate, out_t)


def call(
    body, shapes, args, scalars=0, blocks=0, near_in=0, near_out=0, scratch=(), flops=0, grant=60
):
    hbm, vmem = pl.BlockSpec(memory_space=pltpu.HBM), pl.BlockSpec(memory_space=pltpu.VMEM)
    fixed = scalars + blocks + near_in
    far_in, far_out = args[fixed:], shapes[near_out:]
    moved = sum(x.size * x.dtype.itemsize for x in args)

    def wrapped(*refs):
        ins, rest = refs[: len(args)], refs[len(args) :]
        outs, rest = rest[: len(shapes)], rest[len(shapes) :]
        held_in, rest = rest[: len(far_in)], rest[len(far_in) :]
        held_out, rest = rest[: len(far_out)], rest[len(far_out) :]
        *room, sems = rest
        copies = [
            pltpu.make_async_copy(src, dst, sems.at[i])
            for i, (src, dst) in enumerate(zip(ins[fixed:], held_in))
        ]
        for copy in copies:
            copy.start()
        free = sems.at[pl.ds(len(far_in) + len(far_out), blocks)] if blocks else None

        def ready():
            for copy in copies:
                copy.wait()

        body(ready, free, *ins[:fixed], *held_in, *outs[:near_out], *held_out, *room)
        copies_out = [
            pltpu.make_async_copy(src, dst, sems.at[len(far_in) + i])
            for i, (src, dst) in enumerate(zip(held_out, outs[near_out:]))
        ]
        for copy in copies_out:
            copy.start()
        for copy in copies_out:
            copy.wait()

    room = [pltpu.VMEM(x.shape, x.dtype) for x in far_in]
    room += [pltpu.VMEM(shape, kind) for shape, kind in far_out]
    room += [pltpu.VMEM(shape, kind) for shape, kind in scratch]
    room.append(pltpu.SemaphoreType.DMA((len(far_in) + len(far_out) + blocks,)))
    return pl.pallas_call(
        wrapped,
        out_shape=[jax.ShapeDtypeStruct(shape, kind) for shape, kind in shapes],
        in_specs=[pl.BlockSpec(memory_space=pltpu.SMEM)] * scalars
        + [hbm] * blocks
        + [vmem] * near_in
        + [hbm] * len(far_in),
        out_specs=[vmem] * near_out + [hbm] * len(far_out),
        scratch_shapes=room,
        compiler_params=pltpu.CompilerParams(vmem_limit_bytes=grant << 20),
        cost_estimate=pl.CostEstimate(flops=flops, bytes_accessed=moved, transcendentals=0),
    )(*args)


def dot(a, b, **kw):
    return jnp.dot(a, b, preferred_element_type=F32, **kw)


def iota(shape, dim):
    return lax.broadcasted_iota(jnp.int32, shape, dim)


def one_hot(rows, columns, width, wrap):
    return ((iota((rows, columns), 0) & (wrap - 1)) == iota((rows, columns), 1) // width).astype(BF16)


def spread(x, head_of):
    hi = x.astype(BF16)
    return dot(hi, head_of) + dot((x - hi.astype(F32)).astype(BF16), head_of)


def prompt_start(lengths_ref, positions):
    start, end = jnp.zeros_like(positions), 0
    for i in range(lengths_ref.shape[0]):
        end = end + lengths_ref[i]
        start = jnp.maximum(start, jnp.where(positions >= end, end, 0))
    return start


def lanes(row):
    return jnp.pad(row, ((0, 0), (0, -row.shape[1] % 128)))


def silu(x):
    return x / (1.0 + jnp.exp(-x))


def convolve(rows_ref, at, taps, positions, start):
    tokens, width = positions.shape[0], taps.shape[0]
    total = jnp.zeros(positions.shape, F32)
    for k in range(width):
        back = width - 1 - k
        rows = rows_ref[EDGE - back : EDGE - back + tokens, at : at + positions.shape[1]]
        total = total + jnp.where(positions - back >= start, taps[k : k + 1] * rows, 0.0)
    return silu(total).astype(BF16)


def fetch(blocks, held, sems, columns, order=None):
    depth = blocks[0].shape[0]
    copies = []
    for i, k in enumerate(order or range(len(blocks))):
        copy = pltpu.make_async_copy(
            blocks[k].at[:, columns], held.at[i * depth : (i + 1) * depth], sems.at[i]
        )
        copy.start()
        copies.append(copy)
    return copies


def arrange_body(block_rows, ready, sems, at_ref, order_ref, *refs):
    *pieces, edge_ref, h_ref, held = refs
    ready()
    x_at, core_at, tp_at = at_ref[0], at_ref[1], at_ref[2]
    tokens, features = pieces[0].shape
    x_size, z_size, core_size = SIZES
    for d, piece in enumerate(pieces):
        held[:tokens, d * features : (d + 1) * features] = piece[...]
    held[tokens:] = edge_ref[...]
    wide = h_ref.shape[1]
    each = features // block_rows
    lane = iota((8, wide), 1)
    block = lane // block_rows
    source = lane - block * block_rows
    count = 0
    for turn in range(core_size):
        for d in range(x_size):
            chip = ((x_at + x_size - d) & (x_size - 1)) * z_size
            for z in range(z_size):
                model = order_ref[(chip + z) * core_size + (core_at ^ turn)]
                piece = (tp_at + len(pieces) - model // each) & (len(pieces) - 1)
                base = (piece * each + (model & (each - 1))) * block_rows
                source = source + jnp.where(block == count, base, 0)
                count += 1
    for at in range(0, wide, 256):
        total = jnp.zeros((h_ref.shape[0], 256), F32)
        for k in range(0, wide, features):
            match = iota((features, 256), 0) + k == source[:1, at : at + 256]
            total = total + dot(held[:, k : k + features], match.astype(F32).astype(BF16))
        h_ref[:, at : at + 256] = total.astype(BF16)


def early_body(head_dim, ready, sems, first_ref, lengths_ref, *refs):
    *blocks, h_ref, conv_value, conv_shared, bias, a_log = refs[:-8]
    x_ref, b_ref, dt_ref, cum_ref, sent_ref, held, rows, lines = refs[-8:]
    tokens, inner = x_ref.shape
    copies = fetch(blocks, held, sems, slice(0, held.shape[1]))
    ready()
    for copy in copies:
        copy.wait()
    for at in range(0, held.shape[1], 256):
        part = dot(h_ref[...], held[:, at : at + 256]).astype(BF16).astype(F32)
        rows[EDGE:, at : at + 256] = part[:tokens]
        rows[:EDGE, at : at + 256] = part[tokens:]
    first = first_ref[0]
    positions = first + iota((tokens, 128), 0)
    start = prompt_start(lengths_ref, positions)
    last_start = prompt_start(lengths_ref, first + tokens - 1)
    for at in range(0, inner, 128):
        x_ref[:, at : at + 128] = convolve(
            rows, at, conv_value[:, at : at + 128], positions, start
        )
    b_half = convolve(rows, inner, conv_shared[:, :128], positions, start)
    b_ref[...] = b_half
    raw = rows[EDGE:, inner + 128 :] + lanes(bias[...])
    dt = jnp.maximum(raw, 0.0) + jnp.log1p(jnp.exp(-jnp.abs(raw)))
    below = (iota((tokens, tokens), 0) >= iota((tokens, tokens), 1)).astype(F32)
    cum = dot(below, -dt * jnp.exp(lanes(a_log[...])), precision=lax.Precision.HIGHEST)
    dt_ref[...] = dt
    cum_ref[...] = cum
    last = cum[tokens - 1 :]
    tail = jnp.where(positions >= last_start, jnp.exp(last - cum), 0.0) * dt
    head_of = one_hot(128, inner, head_dim, 128)
    weighted = (spread(tail, head_of) * x_ref[...].astype(F32)).astype(BF16)
    fresh = dot(b_half.astype(F32).T.astype(BF16), weighted)
    lines[...] = jnp.zeros_like(lines)
    count = lines.shape[0] // LINES
    line = 0
    for row in range(0, fresh.shape[0], count):
        for at in range(0, inner, 128):
            lines[pl.ds(line, count, stride=LINES), :] = fresh[row : row + count, at : at + 128]
            line += 1
    keep = jnp.where(last_start < first, jnp.exp(last), 0.0)
    keep = jnp.broadcast_to(keep, (8, 128))
    keep_hi = keep.astype(BF16).astype(F32)
    keep_lo = pltpu.roll(keep - keep_hi, 64, axis=1)
    both = jnp.where(iota((8, 128), 1) < 64, keep_hi, keep_lo)
    lines[pl.ds(line, count, stride=LINES), :] = jnp.concatenate([both] * (count // 8), axis=0)
    sent_ref[...] = lines[...].astype(BF16)


def scan_body(head_dim, inner, copies, ready, sems, sent_ref, out_ref, lines):
    ready()
    lines[...] = sent_ref[...].astype(F32)
    count = lines.shape[0] // LINES
    tiles = inner // 128

    def line(r):
        return lines[pl.ds(r, count, stride=LINES), :]

    keeps = line(copies * tiles).astype(BF16)
    row = iota((count, 128), 0)

    def down(x, d):
        return jnp.where(row >= d, pltpu.roll(x, d, axis=0), 0.0)

    head_of = one_hot(128, inner, head_dim, 64)
    for t in range(tiles):
        keep = dot(keeps, head_of[:, t * 128 : (t + 1) * 128])
        states = [line(i * tiles + t) for i in range(copies)]
        d = 1
        while d < count:
            states = [x + keep * down(x, d) for x in states]
            keep = keep * down(keep, d)
            d *= 2
        for i, x in enumerate(states):
            lines[pl.ds(i * tiles + t, count, stride=LINES), :] = down(x, 1)
    out_ref[...] = lines[...].astype(BF16)


def middle_body(head_dim, ready, sems, first_ref, lengths_ref, core_ref, *refs):
    *blocks, h_ref, conv_shared, x_ref, b_ref, dt_ref, cum_ref, skip = refs[:-7]
    direct_ref, carry_ref, c_ref, out_w, held, c_rows, gate = refs[-7:]
    blocks, deep = blocks[: len(blocks) // 2], blocks[len(blocks) // 2 :]
    tokens, inner = x_ref.shape
    wide = held.shape[1]
    copies = fetch(blocks, held, sems, slice(0, wide))
    ready()
    half = len(deep) // 2
    moves = []
    for i, block in enumerate(deep):
        move = pltpu.make_async_copy(
            block.at[:, :, wide:],
            out_w.at[i % half, :, core_ref[0] ^ (i // half)],
            sems.at[len(deep) + i],
        )
        move.start()
        moves.append(move)
    for copy in copies:
        copy.wait()
    for at in range(0, inner, 256):
        g = dot(h_ref[:tokens], held[:, at : at + 256])
        gate[:, at : at + 256] = silu(g.astype(BF16).astype(F32))
    part = dot(h_ref[...], held[:, inner:]).astype(BF16).astype(F32)
    c_rows[EDGE:] = part[:tokens]
    c_rows[:EDGE] = part[tokens:]
    first = first_ref[0]
    positions = first + iota((tokens, 128), 0)
    start = prompt_start(lengths_ref, positions)
    c_half = convolve(c_rows, 0, conv_shared[:, 128:], positions, start)
    c_ref[...] = c_half
    scores = lax.dot_general(
        c_half, b_ref[...], (((1,), (1,)), ((), ())), preferred_element_type=F32
    )
    i, j = iota((tokens, tokens), 0), iota((tokens, tokens), 1)
    start_wide = jnp.concatenate([start] * (tokens // 128), axis=1)
    scores = jnp.where((j <= i) & (first + j >= start_wide), scores, 0.0)
    dt, cum = dt_ref[...], cum_ref[...]
    head_of = one_hot(128, inner, head_dim, 128)
    stepped = (spread(dt, head_of) * x_ref[...].astype(F32)).astype(BF16)
    cum_t = cum.T
    carry = jnp.where(start < first, jnp.exp(cum), 0.0)
    carry_ref[...] = (spread(carry, head_of) * gate[...]).astype(BF16)
    each = 128 // head_dim
    for at in range(0, inner, 128):
        sums = []
        for h in range(at // head_dim, at // head_dim + each):
            gaps = jnp.minimum(cum[:, h : h + 1] - cum_t[h : h + 1, :], 0.0)
            weights = (jnp.exp(gaps) * scores).astype(BF16)
            sums.append(dot(weights, stepped[:, h * head_dim : (h + 1) * head_dim]))
        cut = slice(at, at + 128)
        direct = jnp.concatenate(sums, axis=1) + skip[:, cut] * x_ref[:, cut].astype(F32)
        direct_ref[:, cut] = (direct * gate[:, cut]).astype(BF16)
    for move in moves:
        move.wait()


def last_body(ready, sems, turn_ref, *refs):
    weight_ref, carried_ref, direct_ref, carry_ref, c_ref, gain = refs[:6]
    *outs, held, lines, shares, out_w = refs[6:]
    weight = pltpu.make_async_copy(weight_ref, out_w, sems.at[0])
    weight.start()
    ready()
    tokens, inner = direct_ref.shape
    lines[...] = carried_ref[...].astype(F32)
    count = lines.shape[0] // LINES
    line = 0
    for row in range(0, held.shape[0], count):
        for at in range(0, inner, 128):
            cut = lines[pl.ds(line, count, stride=LINES), :]
            held[row : row + count, at : at + 128] = cut.astype(BF16)
            line += 1
    direct, carry = direct_ref[...].astype(F32), carry_ref[...].astype(F32)
    gated = direct + carry * dot(c_ref[...], held[...])
    scaled = (gated * gain[...]).astype(BF16)
    nt = (((1,), (1,)), ((), ()))
    features = shares.shape[2]
    weight.wait()
    for i in range(shares.shape[0]):
        rows = out_w[i].reshape(features, inner)
        shares[i] = lax.dot_general(scaled, rows, nt, preferred_element_type=F32).astype(BF16)
    squares = lax.dot_general(
        jnp.ones((8, inner), F32),
        gated * gated,
        nt,
        precision=lax.Precision.HIGHEST,
        preferred_element_type=F32,
    )
    hi = squares.astype(BF16).astype(F32)
    row = iota(squares.shape, 0)
    riding = jnp.where(row == 0, hi, jnp.where(row == 1, squares - hi, 0.0)).astype(BF16)
    for d, out in enumerate(outs):
        out[:tokens] = shares[(turn_ref[0] + len(outs) - d) % len(outs)]
        out[tokens:, :tokens] = riding
        out[tokens:, tokens:] = jnp.zeros((8, features - tokens), BF16)


def on_device(
    hidden_in,
    w_in_gate,
    w_in_value,
    w_in_shared,
    w_in_step,
    conv_value,
    conv_shared,
    dt_bias,
    a_log,
    skip_gain,
    norm_gain,
    w_out,
    prompt_lengths,
    row_blocks,
):
    x_size, z_size, core_size = SIZES
    seq_count = x_size * z_size * core_size
    tp_count = lax.axis_size("tp")
    tokens, features = hidden_in.shape
    rows_here, inner = w_in_value.shape
    shared = w_in_shared.shape[1]
    heads = dt_bias.shape[0]
    head_dim = inner // heads
    state = shared // 2
    x_at, z_at, core_at = (lax.axis_index(name) for name in SEQ)
    tp_at = lax.axis_index("tp")
    seq_at = (x_at * z_size + z_at) * core_size + core_at

    x_shifts = list(range(1, x_size))

    def x_all(block):
        return [block] + [ahead(block, "x", d) for d in x_shifts]

    tie = lax.optimization_barrier

    pieces = [hidden_in] + [ahead(hidden_in, "tp", d) for d in range(1, tp_count)]
    packed = pack(w_in_value, w_in_shared, w_in_step, w_in_gate, w_out.T)
    along_z = lax.all_gather(packed, "z", axis=0, tiled=True)
    early_width = packed.shape[1] - 2 * inner - state
    own = x_all(along_z[:, :early_width])
    late = along_z[:, early_width:]
    edge = jnp.concatenate([piece[tokens - EDGE :] for piece in pieces], axis=1)
    edge = lax.ppermute(edge, SEQ, [(i, i + 1) for i in range(seq_count - 1)])
    rows, model_width = tokens + EDGE, features * tp_count
    (h,) = call(
        functools.partial(arrange_body, rows_here),
        [((rows, model_width), BF16)],
        [jnp.stack([x_at, core_at, tp_at]), row_blocks] + pieces + [edge],
        scalars=2,
        scratch=[((rows, model_width), BF16)],
        flops=2 * rows * model_width * model_width,
    )
    own[-1], h, late = tie((own[-1], h, late))
    other = [ahead(block, "core", 1) for block in own]
    late_own = x_all(late)

    first = jnp.reshape(seq_at * tokens, (1,))
    copies = state // seq_count
    x_rows, b_half, steps, cumulative, sent = call(
        functools.partial(early_body, head_dim),
        [
            ((tokens, inner), BF16),
            ((tokens, state), BF16),
            ((tokens, 128), F32),
            ((tokens, 128), F32),
            ((seq_count * LINES, 128), BF16),
        ],
        [first, prompt_lengths] + own + other + [h, conv_value, conv_shared, dt_bias[None], a_log[None]],
        scalars=2,
        blocks=len(own + other),
        scratch=[
            ((model_width, early_width), BF16),
            ((rows, early_width), F32),
            ((seq_count * LINES, 128), F32),
        ],
        flops=2 * rows * model_width * early_width,
    )
    received = lax.all_to_all(sent.reshape(seq_count, LINES, 128), SEQ, 0, 0, tiled=True)
    (scanned,) = call(
        functools.partial(scan_body, head_dim, inner, copies),
        [((seq_count * LINES, 128), BF16)],
        [received.reshape(seq_count * LINES, 128)],
        near_in=1,
        grant=40,
        scratch=[((seq_count * LINES, 128), F32)],
    )
    carried = lax.all_to_all(scanned.reshape(seq_count, LINES, 128), SEQ, 0, 0, tiled=True)
    carried = carried.reshape(seq_count * LINES, 128)
    late_own, _ = tie((late_own, scanned))
    late_other = [ahead(block, "core", 1) for block in late_own]
    direct, carry, c_half, out_w = call(
        functools.partial(middle_body, head_dim),
        [
            ((tokens, inner), BF16),
            ((tokens, inner), BF16),
            ((tokens, state), BF16),
            ((x_size, z_size, core_size, rows_here, inner), BF16),
        ],
        [first, prompt_lengths, jnp.reshape(core_at, (1,))]
        + late_own
        + late_other
        + [block.reshape(z_size, rows_here, -1) for block in late_own + late_other]
        + [h, conv_shared, x_rows, b_half, steps, cumulative, jnp.repeat(skip_gain, head_dim)[None]],
        scalars=3,
        blocks=2 * len(late_own + late_other),
        near_out=4,
        grant=52,
        scratch=[
            ((model_width, inner + state), BF16),
            ((rows, state), F32),
            ((tokens, inner), F32),
        ],
        flops=2 * rows * model_width * (inner + state),
    )
    shares = call(
        last_body,
        [((tokens + 8, features), BF16)] * tp_count,
        [
            jnp.reshape(x_at - tp_at + tp_count, (1,)),
            out_w,
            carried,
            direct,
            carry,
            c_half,
            norm_gain[None],
        ],
        scalars=1,
        blocks=1,
        near_in=4,
        grant=52,
        scratch=[
            ((state, inner), BF16),
            ((seq_count * LINES, 128), F32),
            ((tp_count, tokens, features), BF16),
            ((x_size, z_size, core_size, rows_here, inner), BF16),
        ],
        flops=2 * tokens * inner * model_width,
    )
    parts = [shares[0]] + [ahead(shares[d], "tp", d) for d in range(1, tp_count)]
    summed = sum(part.astype(F32) for part in parts)
    total = summed[tokens, :tokens] + summed[tokens + 1, :tokens]
    scale = lax.rsqrt(total / (inner * tp_count) + EPSILON)
    return (summed[:tokens] * scale[:, None]).astype(BF16)


def solution(mesh):
    fine = Mesh(mesh.devices.reshape(SIZES + (-1,)), SEQ + ("tp",))
    return jax.shard_map(
        on_device,
        mesh=fine,
        in_specs=(
            P(SEQ, "tp"),
            P(SEQ, "tp"),
            P(SEQ, "tp"),
            P(SEQ, None),
            P(SEQ, "tp"),
            P(None, "tp"),
            P(),
            P("tp"),
            P("tp"),
            P("tp"),
            P("tp"),
            P("tp", SEQ),
            P(),
            P(),
        ),
        out_specs=P(SEQ, "tp"),
        check_vma=False,
    )
```
